128 devices in a mesh: row: 32 (over x, y, core), col: 4 (over z).
Axes of the slice: x: 4, y: 4, z: 4, core: 2. Of those that a mesh axis runs over, the one named last changes fastest.
Arguments:
- start_vectors: float32 [512, 32, 128], P(('row', 'col')), may hold values from -6 to 6
- blocks: bfloat16 [81920, 128, 128], P(('row', 'col')), may hold values from -0.078125 to 0.078125
- block_rows: int32 [81920], P(('row', 'col')), may hold values from 0 to 15
- block_cols: int32 [81920], P(('row', 'col')), may hold values from 0 to 127
- live_counts: int32 [128], P(('row', 'col')), may hold values from 1 to 640, as said below
- center: float32 [], replicated, may hold values from -0.5 to 0.5
- half_width: float32 [], replicated, may hold values from 1.5 to 2.5
Outputs:
- filtered: float32 [512, 32, 128], P(('row', 'col'))
The draws below stay inside these ranges and needn't reach their ends.
Inputs may be any that keep to these rules, and one draw needn't show every extreme that they name: `live_counts`: some device has all 640 slots live.
All inputs are finite; a program needn't handle non-finite values.
Results may differ from the reference program's by a relative error of at most 0.0031.
Values may be sent and summed in bfloat16 or wider, within the bound.
No kernel may reach another device: no remote copies, remote signals or barrier semaphores. Data moves between devices by JAX's collectives and lax.ppermute only.
A program may use at most 64 MiB of HBM per device.

```python
import jax
import jax.numpy as jnp
from jax import lax

BLOCK = 128
NVEC = 32
BLOCKS_DEV = 4
NNZ_DEV = 640
NBLK = 512
SLOTS = 81920
N_ROW = 32
N_COL = 4


def draw_live_counts(key, part):
    key_one, key_two, key_three = jax.random.split(key, 3)
    total = N_ROW * N_COL
    first = jax.random.randint(key_one, (total,), 1, NNZ_DEV + 1)
    second = jax.random.randint(key_two, (total,), 1, NNZ_DEV + 1)
    counts = jnp.maximum(first * second // NNZ_DEV, 1)
    position = jax.random.randint(key_three, (), 0, total)
    return counts.at[position].set(NNZ_DEV).astype(jnp.int32)


def set_ends(values, stream_key, least, top_value):
    spot = [jax.random.randint(jax.random.fold_in(stream_key, axis), (), 0, length) for axis, length in enumerate(values.shape)]
    main_axis = values.shape.index(max(values.shape))
    neighbour = spot[:main_axis] + [(spot[main_axis] + 1) % values.shape[main_axis]] + spot[main_axis + 1:]
    return values.at[tuple(spot)].set(least).at[tuple(neighbour)].set(top_value)


def block_scale(rng, shape, pieces, low, largest):
    gain = 1.0
    for dim, shards_of in pieces:
        steps = jax.random.uniform(jax.random.fold_in(jax.random.fold_in(rng, 6), dim), (shards_of,), jnp.float32, low / len(pieces), largest / len(pieces))
        gain = gain * jnp.repeat(jnp.exp(steps), shape[dim] // shards_of).reshape((-1,) + (1,) * (len(shape) - 1 - dim))
    return gain


def scatter_about(key, shape, width, limit, cuts=(), held_as=jnp.bfloat16):
    array = width * jax.random.normal(key, shape, jnp.float32)
    if cuts:
        array = array * block_scale(key, shape, cuts, -0.22, 0.18)
    return jnp.clip(array, -limit, limit).astype(held_as)


def setup_inputs(seed: int = 0) -> dict:
    key_of = jax.random.split(jax.random.key(seed), 8)
    start_vectors = scatter_about(key_of[0], (NBLK, NVEC, BLOCK), 1.0, 6.0, ((0, 128),), jnp.float32)
    blocks = scatter_about(key_of[1], (SLOTS, BLOCK, BLOCK), (BLOCK * NNZ_DEV // (4 * BLOCKS_DEV)) ** -0.5, 0.078125, ((0, 128),))
    block_rows = set_ends(jax.random.randint(key_of[2], (SLOTS,), 0, N_COL * BLOCKS_DEV), jax.random.fold_in(key_of[2], 1), 0, (N_COL * BLOCKS_DEV) - 1).astype(jnp.int32)
    block_cols = set_ends(jax.random.randint(key_of[3], (SLOTS,), 0, N_ROW * BLOCKS_DEV), jax.random.fold_in(key_of[3], 1), 0, (N_ROW * BLOCKS_DEV) - 1).astype(jnp.int32)
    live_counts = draw_live_counts(jax.random.fold_in(key_of[7], 71), 0)
    center = jnp.clip(jax.random.uniform(key_of[5], (), jnp.float32, -0.5, 0.5), -0.5, 0.5)
    half_width = jnp.clip(jax.random.uniform(key_of[6], (), jnp.float32, 1.5, 2.5), 1.5, 2.5)
    return {"start_vectors": start_vectors, "blocks": blocks, "block_rows": block_rows, "block_cols": block_cols, "live_counts": live_counts, "center": center, "half_width": half_width}


def apply_hamiltonian(vectors, blocks, block_rows, block_cols, live_counts):
    rounded = vectors.astype(jnp.bfloat16).astype(jnp.float32)
    layout = rounded.reshape(N_ROW, N_COL, BLOCKS_DEV, NVEC, BLOCK)
    blocks_grid = blocks.reshape(N_ROW, N_COL, NNZ_DEV, BLOCK, BLOCK)
    rows_grid = block_rows.reshape(N_ROW, N_COL, NNZ_DEV)
    cols_grid = block_cols.reshape(N_ROW, N_COL, NNZ_DEV)
    counts_grid = live_counts.reshape(N_ROW, N_COL)
    slot_ids = jnp.arange(NNZ_DEV, dtype=jnp.int32)

    def per_group(items):
        blocks_here, rows_here, cols_here, counts_here = items
        total = jnp.zeros((N_COL * BLOCKS_DEV, NVEC, BLOCK), jnp.float32)
        for column in range(N_COL):
            group_vec = layout[:, column].reshape(N_ROW * BLOCKS_DEV, NVEC, BLOCK)
            picked = jnp.take(group_vec, cols_here[column], axis=0)
            product = jnp.einsum("bvj,bij->bvi", picked, blocks_here[column].astype(jnp.float32))
            live = (slot_ids < counts_here[column]).astype(jnp.float32)
            product = product * live[:, None, None]
            total = total + jax.ops.segment_sum(product, rows_here[column], num_segments=N_COL * BLOCKS_DEV)
        return total

    result = lax.map(per_group, (blocks_grid, rows_grid, cols_grid, counts_grid))
    return result.reshape(N_ROW * N_COL * BLOCKS_DEV, NVEC, BLOCK)


def reference(start_vectors, blocks, block_rows, block_cols, live_counts, center, half_width):
    first = start_vectors
    second = (apply_hamiltonian(first, blocks, block_rows, block_cols, live_counts) - center * first) / half_width
    third = 2.0 * (apply_hamiltonian(second, blocks, block_rows, block_cols, live_counts) - center * second) / half_width - first
    fourth = 2.0 * (apply_hamiltonian(third, blocks, block_rows, block_cols, live_counts) - center * third) / half_width - second
    return fourth
```

```python
import jax
import jax.numpy as jnp
from jax import lax
from jax.experimental import pallas as pl
from jax.experimental.pallas import tpu as pltpu
from jax.sharding import PartitionSpec as P

SIDE = 4
CORES = 2
CHUNK = 64
UNROLL = 8


def products_kernel(rows, cols, chunks, vec, blocks_hbm, *refs):
    outs, (store, sums, sems) = refs[:-3], refs[-3:]
    n = chunks[0]

    def copy_of(c):
        part = pl.ds(c * CHUNK, CHUNK)
        return pltpu.make_async_copy(blocks_hbm.at[part], store.at[part], sems.at[c])

    @pl.loop(0, n)
    def _(c):
        copy_of(c).start()

    sums[...] = jnp.zeros_like(sums)

    @pl.loop(0, n)
    def _(c):
        copy_of(c).wait()

        @pl.loop(0, CHUNK // UNROLL)
        def _(g):
            first = c * CHUNK + g * UNROLL
            for u in range(UNROLL):
                slot = first + u
                image = lax.dot_general(
                    vec[cols[slot]], store[slot], (((1,), (1,)), ((), ())), preferred_element_type=jnp.float32
                )
                sums[rows[slot]] += image

    owned = outs[0].shape[0]
    for place, out in enumerate(outs):
        out[...] = sums[place * owned : (place + 1) * owned]


def local_products(gathered, blocks, rows, cols, chunks, owned, parts):
    slots, size, _ = blocks.shape
    vecs = gathered.shape[1]
    return pl.pallas_call(
        products_kernel,
        out_shape=[jax.ShapeDtypeStruct((owned, vecs, size), jnp.float32)] * parts,
        grid_spec=pltpu.PrefetchScalarGridSpec(
            num_scalar_prefetch=3,
            grid=(),
            in_specs=[pl.BlockSpec(memory_space=pltpu.VMEM), pl.BlockSpec(memory_space=pl.ANY)],
            out_specs=[pl.BlockSpec(memory_space=pltpu.VMEM)] * parts,
            scratch_shapes=[
                pltpu.VMEM((slots, size, size), jnp.bfloat16),
                pltpu.VMEM((owned * parts + 1, vecs, size), jnp.float32),
                pltpu.SemaphoreType.DMA((slots // CHUNK,)),
            ],
        ),
        cost_estimate=pl.CostEstimate(
            flops=2 * slots * vecs * size * size, bytes_accessed=2 * slots * size * size, transcendentals=0
        ),
    )(rows, cols, chunks, gathered, blocks)


def chip_groups():
    return [[chip * CORES + core for chip in range(SIDE * SIDE)] for core in range(CORES)]


def gathered_vectors(vectors):
    owned = vectors.astype(jnp.bfloat16)
    copies = jnp.broadcast_to(owned, (SIDE * SIDE, *owned.shape))
    mine = lax.all_to_all(copies, "row", 0, 0, tiled=True, axis_index_groups=chip_groups())
    mine = mine.reshape(-1, *owned.shape[1:])
    theirs = lax.ppermute(mine, "row", [(i, i ^ 1) for i in range(SIDE * SIDE * CORES)])
    return jnp.concatenate([mine, theirs])


def on_device(start_vectors, blocks, block_rows, block_cols, live_counts, center, half_width):
    parts = lax.axis_size("col")
    owned = start_vectors.shape[0]
    span = parts * owned
    slots = blocks.shape[0]
    live = live_counts[0]
    here = lax.axis_index("col")
    core = lax.axis_index("row") % CORES

    turned = (block_rows // owned - here) % parts * owned + block_rows % owned
    rows = jnp.where(lax.iota(jnp.int32, slots) < live, turned, span)
    owner = block_cols // owned
    cols = ((owner % CORES) ^ core) * (SIDE * SIDE * owned) + owner // CORES * owned + block_cols % owned
    chunks = ((live + CHUNK - 1) // CHUNK).reshape(1)

    def apply_hamiltonian(vectors):
        pieces = local_products(gathered_vectors(vectors), blocks, rows, cols, chunks, owned, parts)
        total = pieces[0]
        for step in range(1, parts):
            total += lax.ppermute(pieces[step], "col", [(i, (i + step) % parts) for i in range(parts)])
        return total

    second = (apply_hamiltonian(start_vectors) - center * start_vectors) / half_width
    previous, current = (start_vectors, second)
    for turn in range(2):
        image = apply_hamiltonian(current)
        following = 2.0 * (image - center * current) / half_width - previous
        previous, current = (current, following)
    return current


def solution(mesh):
    return jax.shard_map(
        on_device,
        mesh=mesh,
        in_specs=(
            P(("row", "col"), None, None),
            P(("row", "col"), None, None),
            P(("row", "col")),
            P(("row", "col")),
            P(("row", "col")),
            P(),
            P(),
        ),
        out_specs=P(("row", "col"), None, None),
        check_vma=False,
    )
```

```python
import functools

import jax
import jax.numpy as jnp
from jax import lax
from jax.experimental import pallas as pl
from jax.experimental.pallas import tpu as pltpu
from jax.sharding import PartitionSpec as P

SIDE = 4
CORES = 2
CHUNK = 64
UNROLL = 16
GROUP = 8
BATCH = 8
MIB = 1 << 20


VMEM = pl.BlockSpec(memory_space=pltpu.VMEM)
SMEM = pl.BlockSpec(memory_space=pltpu.SMEM)


def small_call(kernel, outs, in_specs, flops=1000):
    cost = pl.CostEstimate(flops=flops, bytes_accessed=1000, transcendentals=0)
    return pl.pallas_call(
        kernel,
        out_shape=outs,
        in_specs=in_specs,
        out_specs=jax.tree.map(lambda _: VMEM, outs),
        compiler_params=pltpu.CompilerParams(vmem_limit_bytes=4 * MIB),
        cost_estimate=cost,
    )


def join_kernel(*refs):
    parts, out = refs[:-1], refs[-1]
    size = parts[0].shape[0]
    for place, part in enumerate(parts):
        out[place * size : (place + 1) * size] = part[...]


def joined(parts):
    shape = (len(parts) * parts[0].shape[0], *parts[0].shape[1:])
    return small_call(join_kernel, jax.ShapeDtypeStruct(shape, parts[0].dtype), [VMEM] * len(parts))(*parts)


def round_kernel(value, out):
    out[...] = value[...].astype(out.dtype)


def rounded(value):
    return small_call(round_kernel, jax.ShapeDtypeStruct(value.shape, jnp.bfloat16), [VMEM])(value)


def chip_shifts(dx, dy, dcore=0):
    pairs = []
    for x in range(SIDE):
        for y in range(SIDE):
            for core in range(CORES):
                to = ((x + dx) % SIDE * SIDE + (y + dy) % SIDE) * CORES + (core + dcore) % CORES
                pairs.append(((x * SIDE + y) * CORES + core, to))
    return pairs


def gathered_vectors(owned):
    line = joined([owned] + [lax.ppermute(owned, "row", chip_shifts(0, dy)) for dy in range(1, SIDE)])
    mine = joined([line] + [lax.ppermute(line, "row", chip_shifts(dx, 0)) for dx in range(1, SIDE)])
    theirs = lax.ppermute(mine, "row", chip_shifts(0, 0, 1))
    return mine, theirs


def padded_room(slots, span):
    step = GROUP * BATCH
    return (slots + span * (GROUP - 1) + step - 1) // step * step


def iota(shape, dim):
    return lax.broadcasted_iota(jnp.int32, shape, dim)


def plan_kernel(parts, owned, live_ref, rows_ref, cols_ref, place_ref, order_ref, groups_ref, sizes_ref):
    live = live_ref[0]
    me, here = lax.axis_index("row"), lax.axis_index("col")
    rows, cols = rows_ref[...], cols_ref[...]
    slots = rows.shape[1]
    span = parts * owned
    room = order_ref.shape[1] - CHUNK
    lanes = groups_ref.shape[1]

    turned = lax.rem(lax.div(rows, owned) + (parts - here), parts) * owned + lax.rem(rows, owned)
    ids = iota((1, slots), 1)
    alive = ids < live
    hot = jnp.where((turned == iota((span, slots), 0)) & alive, 1.0, 0.0)
    earlier = jnp.where(iota((slots, slots), 0) < iota((slots, slots), 1), 1.0, 0.0).astype(jnp.bfloat16)
    rank = jnp.dot(hot.astype(jnp.bfloat16), earlier, preferred_element_type=jnp.float32)
    counts = jnp.sum(hot, axis=1, keepdims=True).astype(jnp.int32)
    padded = lax.div(counts + (GROUP - 1), GROUP) * GROUP
    row_of, lane_of = iota((span, lanes), 0), iota((span, lanes), 1)
    across = jnp.sum(jnp.where(row_of == lane_of, padded, 0).astype(jnp.float32), axis=0, keepdims=True)
    starts = jnp.sum(jnp.where(lane_of < row_of, across, 0.0), axis=1, keepdims=True)
    ends = starts.astype(jnp.int32) + padded
    place = jnp.sum(hot * (rank + starts), axis=0, keepdims=True).astype(jnp.int32)
    place = jnp.where(alive, place, room + lax.rem(ids, CHUNK))
    place_ref[...] = place

    owner = lax.div(cols, owned)
    chip, my_chip = lax.div(owner, CORES), lax.div(me, CORES)
    dx = lax.rem(lax.div(my_chip, SIDE) + SIDE - lax.div(chip, SIDE), SIDE)
    dy = lax.rem(lax.rem(my_chip, SIDE) + SIDE - lax.rem(chip, SIDE), SIDE)
    dcore = lax.rem(me + owner, CORES)
    source = ((dcore * SIDE + dx) * SIDE + dy) * owned + lax.rem(cols, owned)
    absent = SIDE * SIDE * CORES * owned
    weights = jnp.broadcast_to(jnp.where(alive, source - absent, 0).astype(jnp.float32), (8, slots)).astype(jnp.bfloat16)
    for block in range((room + CHUNK) // CHUNK):
        match = jnp.where(place == iota((CHUNK, slots), 0) + block * CHUNK, 1.0, 0.0).astype(jnp.bfloat16)
        found = lax.dot_general(weights, match, (((1,), (1,)), ((), ())), preferred_element_type=jnp.float32)
        order_ref[:, block * CHUNK : (block + 1) * CHUNK] = found[:1].astype(jnp.int32) + absent

    ended = jnp.where(ends <= lane_of * GROUP, 1.0, 0.0)
    groups_ref[...] = jnp.sum(ended, axis=0, keepdims=True).astype(jnp.int32)
    total = jnp.sum(padded.astype(jnp.float32), axis=0, keepdims=True).astype(jnp.int32)
    at_ends = jnp.sum(jnp.where(row_of == lane_of, ends, 0).astype(jnp.float32), axis=0, keepdims=True).astype(jnp.int32)
    lane = iota((1, lanes), 1)
    batches = lax.div(total + (GROUP * BATCH - 1), GROUP * BATCH)
    sizes = jnp.where(lane == span, lax.div(live + (CHUNK - 1), CHUNK), at_ends)
    sizes = jnp.where(lane == span + 1, batches, sizes)
    sizes_ref[...] = jnp.where(lane == span + 2, total, sizes)


def sort_plan(rows, cols, live, parts, owned):
    slots = rows.shape[0]
    room = padded_room(slots, parts * owned)
    widths = (slots, room + CHUNK, 128, 128)
    return pl.pallas_call(
        functools.partial(plan_kernel, parts, owned),
        out_shape=[jax.ShapeDtypeStruct((1, width), jnp.int32) for width in widths],
        in_specs=[SMEM, VMEM, VMEM],
        out_specs=[VMEM] * len(widths),
        compiler_params=pltpu.CompilerParams(vmem_limit_bytes=8 * MIB),
        cost_estimate=pl.CostEstimate(flops=1000, bytes_accessed=1000, transcendentals=0),
    )(live, rows.reshape(1, slots), cols.reshape(1, slots))


def prepare_kernel(span, place, sizes, _center, _half, blocks_hbm, store, raw, sems):
    chunks = sizes[0, span]
    total = sizes[0, span + 2]
    room = store.shape[0] - CHUNK
    size = raw.shape[1]

    def copy_of(c):
        part = pl.ds(c * CHUNK, CHUNK)
        return pltpu.make_async_copy(blocks_hbm.at[part], raw.at[part], sems.at[c])

    @pl.loop(0, chunks)
    def _(c):
        copy_of(c).start()

    nothing = jnp.zeros((GROUP, size, size), store.dtype)

    @pl.loop(0, span)
    def _(row):
        store[pl.ds(jnp.maximum(sizes[0, row] - GROUP, 0), GROUP)] = nothing

    @pl.loop(0, BATCH)
    def _(k):
        @pl.when(total + k * GROUP < room)
        def _():
            store[pl.ds(total + k * GROUP, GROUP)] = nothing

    @pl.loop(0, chunks)
    def _(c):
        copy_of(c).wait()

        @pl.loop(0, CHUNK // UNROLL)
        def _(g):
            for u in range(UNROLL):
                slot = c * CHUNK + g * UNROLL + u
                store[place[0, slot]] = raw[slot].T


def prepared(place, sizes, blocks, scalars, span):
    slots, size, _ = blocks.shape
    return pl.pallas_call(
        functools.partial(prepare_kernel, span),
        out_shape=pltpu.VMEM((padded_room(slots, span) + CHUNK, size, size), blocks.dtype),
        in_specs=[SMEM] * 4 + [pl.BlockSpec(memory_space=pl.ANY)],
        out_specs=VMEM,
        scratch_shapes=[
            pltpu.VMEM((slots, size, size), blocks.dtype),
            pltpu.SemaphoreType.DMA((slots // CHUNK,)),
        ],
        compiler_params=pltpu.CompilerParams(vmem_limit_bytes=24 * MIB),
        cost_estimate=pl.CostEstimate(flops=1000, bytes_accessed=2 * slots * size * size, transcendentals=0),
    )(place, sizes, *scalars, blocks)


def products_kernel(order, group_rows, sizes, mine, theirs, store, *refs):
    outs, (vec, sums) = refs[:-2], refs[-2:]
    half = mine.shape[0]
    size = store.shape[1]
    vec[:half] = mine[...]
    vec[half : 2 * half] = theirs[...]
    vec[2 * half] = jnp.zeros_like(vec[2 * half])
    sums[...] = jnp.zeros_like(sums)

    @pl.loop(0, sizes[0, sums.shape[0]])
    def _(batch):
        for k in range(BATCH):
            group = batch * BATCH + k
            left = jnp.concatenate([vec[order[0, group * GROUP + i]] for i in range(GROUP)], axis=1)
            right = store[pl.ds(group * GROUP, GROUP)].reshape(GROUP * size, size)
            sums[group_rows[0, group]] += jnp.dot(left, right, preferred_element_type=jnp.float32)

    owned = outs[0].shape[0]
    for place, out in enumerate(outs):
        out[...] = sums[place * owned : (place + 1) * owned]


def local_products(gathered, prep, owned, parts):
    order, group_rows, sizes, store = prep
    mine, theirs = gathered
    half, vecs, size = mine.shape
    return pl.pallas_call(
        products_kernel,
        out_shape=[jax.ShapeDtypeStruct((owned, vecs, size), jnp.float32)] * parts,
        in_specs=[SMEM, SMEM, SMEM, VMEM, VMEM, VMEM],
        out_specs=[VMEM] * parts,
        scratch_shapes=[
            pltpu.VMEM((2 * half + 1, vecs, size), jnp.bfloat16),
            pltpu.VMEM((owned * parts + 1, vecs, size), jnp.float32),
        ],
        compiler_params=pltpu.CompilerParams(vmem_limit_bytes=8 * MIB),
        cost_estimate=pl.CostEstimate(flops=2 * 640 * vecs * size * size, bytes_accessed=2 * MIB, transcendentals=0),
    )(order, group_rows, sizes, mine, theirs, pltpu.with_memory_space_constraint(store, pltpu.VMEM))


def first_kernel(center, half_width, current, *refs):
    pieces, (out, out_bf) = refs[:-2], refs[-2:]
    image = pieces[0][...]
    for piece in pieces[1:]:
        image += piece[...]
    value = (image - center[0] * current[...]) / half_width[0]
    out[...] = value
    out_bf[...] = value.astype(out_bf.dtype)


def next_kernel(center, half_width, current, previous, *refs):
    pieces, (out, out_bf) = refs[:-2], refs[-2:]
    image = pieces[0][...]
    for piece in pieces[1:]:
        image += piece[...]
    value = 2.0 * (image - center[0] * current[...]) / half_width[0] - previous[...]
    out[...] = value
    out_bf[...] = value.astype(out_bf.dtype)


def on_device(start_vectors, blocks, block_rows, block_cols, live_counts, center, half_width):
    parts = lax.axis_size("col")
    owned = start_vectors.shape[0]
    shape = start_vectors.shape
    scalars = (center.reshape(1), half_width.reshape(1))
    place, order, group_rows, sizes = sort_plan(block_rows, block_cols, live_counts, parts, owned)
    prep = (order, group_rows, sizes, prepared(place, sizes, blocks, scalars, parts * owned))
    outs = (jax.ShapeDtypeStruct(shape, jnp.float32), jax.ShapeDtypeStruct(shape, jnp.bfloat16))

    def image_pieces(rounded_vectors):
        pieces = local_products(gathered_vectors(rounded_vectors), prep, owned, parts)
        sent = [lax.ppermute(pieces[s], "col", [(i, (i + s) % parts) for i in range(parts)]) for s in range(1, parts)]
        return [pieces[0], *sent]

    pieces = image_pieces(rounded(start_vectors))
    first = small_call(first_kernel, outs, [SMEM, SMEM] + [VMEM] * (1 + parts))
    current, current_bf = first(*scalars, start_vectors, *pieces)
    previous = start_vectors
    for turn in range(2):
        pieces = image_pieces(current_bf)
        step = small_call(next_kernel, outs, [SMEM, SMEM] + [VMEM] * (2 + parts))
        following, current_bf = step(*scalars, current, previous, *pieces)
        previous, current = current, following
    return current


def solution(mesh):
    return jax.shard_map(
        on_device,
        mesh=mesh,
        in_specs=(
            P(("row", "col"), None, None),
            P(("row", "col"), None, None),
            P(("row", "col")),
            P(("row", "col")),
            P(("row", "col")),
            P(),
            P(),
        ),
        out_specs=P(("row", "col"), None, None),
        check_vma=False,
    )
```

```python
import functools

import jax
import jax.numpy as jnp
from jax import lax
from jax.experimental import pallas as pl
from jax.experimental.pallas import tpu as pltpu
from jax.sharding import PartitionSpec as P


SIDE = 4
CORES = 2
CHUNK = 64
UNROLL = 16
GROUP = 8
BATCH = 4
MIB = 1 << 20


VMEM = pl.BlockSpec(memory_space=pltpu.VMEM)
SMEM = pl.BlockSpec(memory_space=pltpu.SMEM)


def small_call(kernel, outs, in_specs, flops=1000):
    cost = pl.CostEstimate(flops=flops, bytes_accessed=1000, transcendentals=0)
    return pl.pallas_call(
        kernel,
        out_shape=outs,
        in_specs=in_specs,
        out_specs=jax.tree.map(lambda _: VMEM, outs),
        compiler_params=pltpu.CompilerParams(vmem_limit_bytes=4 * MIB),
        cost_estimate=cost,
    )


def join_kernel(count, *refs):
    parts, out = refs[:count], refs[-1]
    size = parts[0].shape[0]
    for place, part in enumerate(parts):
        out[place * size : (place + 1) * size] = part[...]


def joined(parts, after=()):
    shape = (len(parts) * parts[0].shape[0], *parts[0].shape[1:])
    kernel = functools.partial(join_kernel, len(parts))
    specs = [VMEM] * (len(parts) + len(after))
    return small_call(kernel, jax.ShapeDtypeStruct(shape, parts[0].dtype), specs)(*parts, *after)


def round_kernel(value, out):
    out[...] = value[...].astype(out.dtype)


def rounded(value):
    return small_call(round_kernel, jax.ShapeDtypeStruct(value.shape, jnp.bfloat16), [VMEM])(value)


def chip_shifts(dx, dy, dcore=0):
    pairs = []
    for x in range(SIDE):
        for y in range(SIDE):
            for core in range(CORES):
                to = ((x + dx) % SIDE * SIDE + (y + dy) % SIDE) * CORES + (core + dcore) % CORES
                pairs.append(((x * SIDE + y) * CORES + core, to))
    return pairs


def line_gathered(owned, after=()):
    return joined([owned] + [lax.ppermute(owned, "row", chip_shifts(0, dy)) for dy in range(1, SIDE)], after)


def all_gathered(line, after=()):
    mine = joined([line] + [lax.ppermute(line, "row", chip_shifts(dx, 0)) for dx in range(1, SIDE)], after)
    theirs = lax.ppermute(mine, "row", chip_shifts(0, 0, 1))
    return joined([mine, theirs])


def padded_room(slots, span):
    step = GROUP * BATCH
    return (slots + span * (GROUP - 1) + step - 1) // step * step


def iota(shape, dim):
    return lax.broadcasted_iota(jnp.int32, shape, dim)


def plan_kernel(parts, owned, live_ref, rows_ref, cols_ref, _after, place_ref, order_ref, groups_ref, sizes_ref):
    live = live_ref[0]
    me, here = lax.axis_index("row"), lax.axis_index("col")
    rows, cols = rows_ref[...], cols_ref[...]
    slots = rows.shape[1]
    span = parts * owned
    room = order_ref.shape[1] - CHUNK
    lanes = groups_ref.shape[1]

    turned = lax.rem(lax.div(rows, owned) + (parts - here), parts) * owned + lax.rem(rows, owned)
    ids = iota((1, slots), 1)
    alive = ids < live
    hot = jnp.where((turned == iota((span, slots), 0)) & alive, 1.0, 0.0)
    earlier = jnp.where(iota((slots, slots), 0) < iota((slots, slots), 1), 1.0, 0.0).astype(jnp.bfloat16)
    rank = jnp.dot(hot.astype(jnp.bfloat16), earlier, preferred_element_type=jnp.float32)
    counts = jnp.sum(hot, axis=1, keepdims=True).astype(jnp.int32)
    padded = lax.div(counts + (GROUP - 1), GROUP) * GROUP
    row_of, lane_of = iota((span, lanes), 0), iota((span, lanes), 1)
    across = jnp.sum(jnp.where(row_of == lane_of, padded, 0).astype(jnp.float32), axis=0, keepdims=True)
    starts = jnp.sum(jnp.where(lane_of < row_of, across, 0.0), axis=1, keepdims=True)
    ends = starts.astype(jnp.int32) + padded
    place = jnp.sum(hot * (rank + starts), axis=0, keepdims=True).astype(jnp.int32)
    place = jnp.where(alive, place, room + lax.rem(ids, CHUNK))
    place_ref[...] = place

    owner = lax.div(cols, owned)
    chip, my_chip = lax.div(owner, CORES), lax.div(me, CORES)
    dx = lax.rem(lax.div(my_chip, SIDE) + SIDE - lax.div(chip, SIDE), SIDE)
    dy = lax.rem(lax.rem(my_chip, SIDE) + SIDE - lax.rem(chip, SIDE), SIDE)
    dcore = lax.rem(me + owner, CORES)
    source = ((dcore * SIDE + dx) * SIDE + dy) * owned + lax.rem(cols, owned)
    weights = jnp.broadcast_to(jnp.where(alive, source, 0).astype(jnp.float32), (8, slots)).astype(jnp.bfloat16)
    for block in range((room + CHUNK) // CHUNK):
        match = jnp.where(place == iota((CHUNK, slots), 0) + block * CHUNK, 1.0, 0.0).astype(jnp.bfloat16)
        found = lax.dot_general(weights, match, (((1,), (1,)), ((), ())), preferred_element_type=jnp.float32)
        order_ref[:, block * CHUNK : (block + 1) * CHUNK] = found[:1].astype(jnp.int32)

    ended = jnp.where(ends <= lane_of * GROUP, 1.0, 0.0)
    groups_ref[...] = jnp.sum(ended, axis=0, keepdims=True).astype(jnp.int32)
    total = jnp.sum(padded.astype(jnp.float32), axis=0, keepdims=True).astype(jnp.int32)
    at_ends = jnp.sum(jnp.where(row_of == lane_of, ends, 0).astype(jnp.float32), axis=0, keepdims=True).astype(jnp.int32)
    lane = iota((1, lanes), 1)
    batches = lax.div(total + (GROUP * BATCH - 1), GROUP * BATCH)
    sizes = jnp.where(lane == span, lax.div(live + (CHUNK - 1), CHUNK), at_ends)
    sizes = jnp.where(lane == span + 1, batches, sizes)
    sizes_ref[...] = jnp.where(lane == span + 2, total, sizes)


def sort_plan(rows, cols, live, after, parts, owned):
    slots = rows.shape[0]
    room = padded_room(slots, parts * owned)
    widths = (slots, room + CHUNK, 128, 128)
    return pl.pallas_call(
        functools.partial(plan_kernel, parts, owned),
        out_shape=[jax.ShapeDtypeStruct((1, width), jnp.int32) for width in widths],
        in_specs=[SMEM, VMEM, VMEM, VMEM],
        out_specs=[VMEM] * len(widths),
        compiler_params=pltpu.CompilerParams(vmem_limit_bytes=8 * MIB),
        cost_estimate=pl.CostEstimate(flops=1000, bytes_accessed=1000, transcendentals=0),
    )(live, rows.reshape(1, slots), cols.reshape(1, slots), after)


def prepare_kernel(span, place, sizes, _center, _half, _after, blocks_hbm, store, raw, sems):
    chunks = sizes[0, span]
    total = sizes[0, span + 2]
    room = store.shape[0] - CHUNK
    size = raw.shape[1]

    def copy_of(c):
        part = pl.ds(c * CHUNK, CHUNK)
        return pltpu.make_async_copy(blocks_hbm.at[part], raw.at[part], sems.at[c])

    @pl.loop(0, chunks)
    def _(c):
        copy_of(c).start()

    nothing = jnp.zeros((GROUP, size, size), store.dtype)

    @pl.loop(0, span)
    def _(row):
        store[pl.ds(jnp.maximum(sizes[0, row] - GROUP, 0), GROUP)] = nothing

    @pl.loop(0, BATCH)
    def _(k):
        @pl.when(total + k * GROUP < room)
        def _():
            store[pl.ds(total + k * GROUP, GROUP)] = nothing

    @pl.loop(0, chunks)
    def _(c):
        copy_of(c).wait()

        @pl.loop(0, CHUNK // UNROLL)
        def _(g):
            for u in range(UNROLL):
                slot = c * CHUNK + g * UNROLL + u
                store[place[0, slot]] = raw[slot].T


def prepared(place, sizes, blocks, scalars, after, span):
    slots, size, _ = blocks.shape
    return pl.pallas_call(
        functools.partial(prepare_kernel, span),
        out_shape=pltpu.VMEM((padded_room(slots, span) + CHUNK, size, size), blocks.dtype),
        in_specs=[SMEM] * 4 + [VMEM, pl.BlockSpec(memory_space=pl.ANY)],
        out_specs=VMEM,
        scratch_shapes=[
            pltpu.VMEM((slots, size, size), blocks.dtype),
            pltpu.SemaphoreType.DMA((slots // CHUNK,)),
        ],
        compiler_params=pltpu.CompilerParams(vmem_limit_bytes=24 * MIB),
        cost_estimate=pl.CostEstimate(flops=1000, bytes_accessed=2 * slots * size * size, transcendentals=0),
    )(place, sizes, *scalars, after, blocks)


def products_kernel(first_row, order, groups, sizes, vec, store, *refs):
    out, sums = refs[-2:]
    owned = out.shape[0]
    size = store.shape[1]
    start = lax.div(sizes[0, first_row - 1], GROUP) if first_row else 0
    count = lax.div(sizes[0, first_row + owned - 1], GROUP) - start
    sums[...] = jnp.zeros_like(sums)

    @pl.loop(0, lax.div(count + (BATCH - 1), BATCH))
    def _(batch):
        for k in range(BATCH):
            group = start + batch * BATCH + k
            left = jnp.concatenate([vec[order[0, group * GROUP + i]] for i in range(GROUP)], axis=1)
            right = store[pl.ds(group * GROUP, GROUP)].reshape(GROUP * size, size)
            sums[groups[0, group]] += jnp.dot(left, right, preferred_element_type=jnp.float32)

    out[...] = sums[first_row : first_row + owned]


def local_products(part, vec, prep, after, owned, parts):
    order, groups, sizes, store = prep
    _, vecs, size = vec.shape
    return pl.pallas_call(
        functools.partial(products_kernel, part * owned),
        out_shape=jax.ShapeDtypeStruct((owned, vecs, size), jnp.float32),
        in_specs=[SMEM] * 3 + [VMEM] * (2 + len(after)),
        out_specs=VMEM,
        scratch_shapes=[pltpu.VMEM((owned * parts + 1, vecs, size), jnp.float32)],
        compiler_params=pltpu.CompilerParams(vmem_limit_bytes=4 * MIB),
        cost_estimate=pl.CostEstimate(flops=640 // 2 * vecs * size * size, bytes_accessed=MIB, transcendentals=0),
    )(order, groups, sizes, vec, kept(store), *after)


def kept(store):
    return pltpu.with_memory_space_constraint(store, pltpu.VMEM)


def first_kernel(center, half_width, current, *refs):
    pieces, (out, out_bf) = refs[:-2], refs[-2:]
    image = pieces[0][...]
    for piece in pieces[1:]:
        image += piece[...]
    value = (image - center[0] * current[...]) / half_width[0]
    out[...] = value
    out_bf[...] = value.astype(out_bf.dtype)


def next_kernel(center, half_width, current, previous, *refs):
    pieces, (out, out_bf) = refs[:-2], refs[-2:]
    image = pieces[0][...]
    for piece in pieces[1:]:
        image += piece[...]
    value = 2.0 * (image - center[0] * current[...]) / half_width[0] - previous[...]
    out[...] = value
    out_bf[...] = value.astype(out_bf.dtype)


def on_device(start_vectors, blocks, block_rows, block_cols, live_counts, center, half_width):
    parts = lax.axis_size("col")
    owned = start_vectors.shape[0]
    shape = start_vectors.shape
    scalars = (center.reshape(1), half_width.reshape(1))
    outs = (jax.ShapeDtypeStruct(shape, jnp.float32), jax.ShapeDtypeStruct(shape, jnp.bfloat16))

    def image_pieces(vec):
        pieces, last = [], ()
        for part in (*range(1, parts), 0):
            piece = local_products(part, vec, prep, last, owned, parts)
            last = (piece,)
            if part:
                piece = lax.ppermute(piece, "col", [(i, (i + part) % parts) for i in range(parts)])
            pieces.append(piece)
        return pieces

    start_bf = rounded(start_vectors)
    place, order, groups, sizes = sort_plan(block_rows, block_cols, live_counts, start_bf, parts, owned)
    line = line_gathered(start_bf, (sizes,))
    store = prepared(place, sizes, blocks, scalars, line, parts * owned)
    prep = (order, groups, sizes, store)
    pieces = image_pieces(all_gathered(line, (kept(store),)))
    first = small_call(first_kernel, outs, [SMEM, SMEM] + [VMEM] * (1 + parts))
    current, current_bf = first(*scalars, start_vectors, *pieces)
    previous = start_vectors
    for _ in range(2):
        pieces = image_pieces(all_gathered(line_gathered(current_bf)))
        step = small_call(next_kernel, outs, [SMEM, SMEM] + [VMEM] * (2 + parts))
        following, current_bf = step(*scalars, current, previous, *pieces)
        previous, current = current, following
    return current


def solution(mesh):
    return jax.shard_map(
        on_device,
        mesh=mesh,
        in_specs=(
            P(("row", "col"), None, None),
            P(("row", "col"), None, None),
            P(("row", "col")),
            P(("row", "col")),
            P(("row", "col")),
            P(),
            P(),
        ),
        out_specs=P(("row", "col"), None, None),
        check_vma=False,
    )
```

```python
import functools

import jax
import jax.numpy as jnp
from jax import lax
from jax.experimental import pallas as pl
from jax.experimental.pallas import tpu as pltpu
from jax.sharding import PartitionSpec as P


SIDE = 4
CORES = 2
CHUNK = 32
SPARE = 64
GROUP = 4
BATCH = 24
LANES = 256
HEAD = 2 * LANES
MIB = 1 << 20


VMEM = pl.BlockSpec(memory_space=pltpu.VMEM)
SMEM = pl.BlockSpec(memory_space=pltpu.SMEM)


def small_call(kernel, outs, in_specs, flops=1000):
    cost = pl.CostEstimate(flops=flops, bytes_accessed=1000, transcendentals=0)
    return pl.pallas_call(
        kernel,
        out_shape=outs,
        in_specs=in_specs,
        out_specs=jax.tree.map(lambda _: VMEM, outs),
        compiler_params=pltpu.CompilerParams(vmem_limit_bytes=4 * MIB),
        cost_estimate=cost,
    )


def join_kernel(count, *refs):
    parts, out = refs[:count], refs[-1]
    size = parts[0].shape[0]
    for place, part in enumerate(parts):
        out[place * size : (place + 1) * size] = part[...]


def joined(parts, after=(), after_specs=()):
    shape = (len(parts) * parts[0].shape[0], *parts[0].shape[1:])
    kernel = functools.partial(join_kernel, len(parts))
    specs = [VMEM] * len(parts) + list(after_specs or [VMEM] * len(after))
    return small_call(kernel, jax.ShapeDtypeStruct(shape, parts[0].dtype), specs)(*parts, *after)


def round_kernel(value, out):
    out[...] = value[...].astype(out.dtype)


def rounded(value):
    return small_call(round_kernel, jax.ShapeDtypeStruct(value.shape, jnp.bfloat16), [VMEM])(value)


def chip_shifts(dx, dy, dcore=0):
    pairs = []
    for x in range(SIDE):
        for y in range(SIDE):
            for core in range(CORES):
                to = ((x + dx) % SIDE * SIDE + (y + dy) % SIDE) * CORES + (core + dcore) % CORES
                pairs.append(((x * SIDE + y) * CORES + core, to))
    return pairs


def line_gathered(owned, after=(), specs=()):
    return joined([owned] + [lax.ppermute(owned, "row", chip_shifts(0, dy)) for dy in range(1, SIDE)], after, specs)


def all_gathered(line, after=()):
    mine = joined([line] + [lax.ppermute(line, "row", chip_shifts(dx, 0)) for dx in range(1, SIDE)], after)
    theirs = lax.ppermute(mine, "row", chip_shifts(0, 0, 1))
    return joined([mine, theirs])


def padded_room(slots, span):
    step = GROUP * BATCH
    return (slots + span * (GROUP - 1) + step - 1) // step * step


def iota(shape, dim):
    return lax.broadcasted_iota(jnp.int32, shape, dim)


def plan_kernel(parts, owned, live_ref, rows_ref, cols_ref, _center, _half, _after, place_out, table_out, place_ref, table_ref, sems):
    live = live_ref[0]
    me, here = lax.axis_index("row"), lax.axis_index("col")
    rows, cols = rows_ref[...], cols_ref[...]
    slots = rows.shape[1]
    span = parts * owned
    lanes = LANES
    head = HEAD
    room = table_ref.shape[1] - head - SPARE

    turned = lax.rem(lax.div(rows, owned) + (parts - here), parts) * owned + lax.rem(rows, owned)
    ids = iota((1, slots), 1)
    alive = ids < live
    hot = jnp.where((turned == iota((span, slots), 0)) & alive, 1.0, 0.0)
    earlier = jnp.where(iota((slots, slots), 0) < iota((slots, slots), 1), 1.0, 0.0).astype(jnp.bfloat16)
    rank = jnp.dot(hot.astype(jnp.bfloat16), earlier, preferred_element_type=jnp.float32)
    counts = jnp.sum(hot, axis=1, keepdims=True).astype(jnp.int32)
    padded = lax.div(counts + (GROUP - 1), GROUP) * GROUP
    row_of, lane_of = iota((span, lanes), 0), iota((span, lanes), 1)
    across = jnp.sum(jnp.where(row_of == lane_of, padded, 0).astype(jnp.float32), axis=0, keepdims=True)
    starts = jnp.sum(jnp.where(lane_of < row_of, across, 0.0), axis=1, keepdims=True)
    ends = starts.astype(jnp.int32) + padded
    place = jnp.sum(hot * (rank + starts), axis=0, keepdims=True).astype(jnp.int32)
    place = jnp.where(alive, place, room + lax.rem(ids, CHUNK))
    place_ref[...] = place

    owner = lax.div(cols, owned)
    chip, my_chip = lax.div(owner, CORES), lax.div(me, CORES)
    dx = lax.rem(lax.div(my_chip, SIDE) + SIDE - lax.div(chip, SIDE), SIDE)
    dy = lax.rem(lax.rem(my_chip, SIDE) + SIDE - lax.rem(chip, SIDE), SIDE)
    dcore = lax.rem(me + owner, CORES)
    source = ((dcore * SIDE + dx) * SIDE + dy) * owned + lax.rem(cols, owned)
    weights = jnp.broadcast_to(jnp.where(alive, source, 0).astype(jnp.float32), (8, slots)).astype(jnp.bfloat16)
    for block in range((room + SPARE) // SPARE):
        match = jnp.where(place == iota((SPARE, slots), 0) + block * SPARE, 1.0, 0.0).astype(jnp.bfloat16)
        found = lax.dot_general(weights, match, (((1,), (1,)), ((), ())), preferred_element_type=jnp.float32)
        table_ref[:, head + block * SPARE : head + (block + 1) * SPARE] = found[:1].astype(jnp.int32)

    ended = jnp.where(ends <= lane_of * GROUP, 1.0, 0.0)
    table_ref[:, lanes:head] = jnp.sum(ended, axis=0, keepdims=True).astype(jnp.int32)
    at_ends = jnp.sum(jnp.where(row_of == lane_of, ends, 0).astype(jnp.float32), axis=0, keepdims=True).astype(jnp.int32)
    lane = iota((1, lanes), 1)
    table_ref[:, :lanes] = jnp.where(lane == span, lax.div(live + (CHUNK - 1), CHUNK), at_ends)
    copies = [
        pltpu.make_async_copy(place_ref, place_out, sems.at[0]),
        pltpu.make_async_copy(table_ref, table_out, sems.at[1]),
    ]
    for copy in copies:
        copy.start()
    for copy in copies:
        copy.wait()


def sort_plan(rows, cols, live, scalars, after, parts, owned):
    slots = rows.shape[0]
    room = padded_room(slots, parts * owned)
    widths = (slots, HEAD + room + SPARE)
    return pl.pallas_call(
        functools.partial(plan_kernel, parts, owned),
        out_shape=[pltpu.SMEM((1, width), jnp.int32) for width in widths],
        in_specs=[SMEM, VMEM, VMEM, SMEM, SMEM, VMEM],
        out_specs=[SMEM] * len(widths),
        scratch_shapes=[pltpu.VMEM((1, width), jnp.int32) for width in widths] + [pltpu.SemaphoreType.DMA((2,))],
        compiler_params=pltpu.CompilerParams(vmem_limit_bytes=8 * MIB),
        cost_estimate=pl.CostEstimate(flops=1000, bytes_accessed=1000, transcendentals=0),
    )(live, rows.reshape(1, slots), cols.reshape(1, slots), *scalars, after)


def prepare_kernel(span, place, sizes, _after, blocks_hbm, store, raw, sems):
    chunks = sizes[0, span]
    size = raw.shape[1]

    def copy_of(c):
        part = pl.ds(c * CHUNK, CHUNK)
        return pltpu.make_async_copy(blocks_hbm.at[part], raw.at[part], sems.at[c])

    @pl.loop(0, chunks)
    def _(c):
        copy_of(c).start()

    nothing = jnp.zeros((GROUP, size, size), store.dtype)

    @pl.loop(0, span)
    def _(row):
        store[pl.ds(jnp.maximum(sizes[0, row] - GROUP, 0), GROUP)] = nothing

    @pl.loop(0, chunks)
    def _(c):
        copy_of(c).wait()

        for u in range(CHUNK):
            slot = c * CHUNK + u
            store[place[0, slot]] = raw[slot].T


def prepared(place, sizes, blocks, after, span):
    slots, size, _ = blocks.shape
    return pl.pallas_call(
        functools.partial(prepare_kernel, span),
        out_shape=pltpu.VMEM((padded_room(slots, span) + SPARE, size, size), blocks.dtype),
        in_specs=[SMEM] * 2 + [VMEM, pl.BlockSpec(memory_space=pl.ANY)],
        out_specs=VMEM,
        scratch_shapes=[
            pltpu.VMEM((slots, size, size), blocks.dtype),
            pltpu.SemaphoreType.DMA((slots // CHUNK,)),
        ],
        compiler_params=pltpu.CompilerParams(vmem_limit_bytes=24 * MIB),
        cost_estimate=pl.CostEstimate(flops=1000, bytes_accessed=2 * slots * size * size, transcendentals=0),
    )(place, sizes, after, blocks)


def products_kernel(first_row, table, vec, store, *refs):
    out, sums = refs[-2:]
    owned = out.shape[0]
    size = store.shape[1]
    start = lax.div(table[0, first_row - 1], GROUP) if first_row else 0
    count = lax.div(table[0, first_row + owned - 1], GROUP) - start
    sums[...] = jnp.zeros_like(sums)

    @pl.loop(0, lax.div(count + (BATCH - 1), BATCH))
    def _(batch):
        for k in range(BATCH):
            group = start + batch * BATCH + k
            left = jnp.concatenate([vec[table[0, HEAD + group * GROUP + i]] for i in range(GROUP)], axis=1)
            right = store[pl.ds(group * GROUP, GROUP)].reshape(GROUP * size, size)
            sums[table[0, LANES + group]] += jnp.dot(left, right, preferred_element_type=jnp.float32)

    out[...] = sums[first_row : first_row + owned]


def local_products(part, vec, prep, after, owned, parts):
    table, store = prep
    _, vecs, size = vec.shape
    return pl.pallas_call(
        functools.partial(products_kernel, part * owned),
        out_shape=jax.ShapeDtypeStruct((owned, vecs, size), jnp.float32),
        in_specs=[SMEM] + [VMEM] * (2 + len(after)),
        out_specs=VMEM,
        scratch_shapes=[pltpu.VMEM((owned * parts + 1, vecs, size), jnp.float32)],
        compiler_params=pltpu.CompilerParams(vmem_limit_bytes=4 * MIB),
        cost_estimate=pl.CostEstimate(flops=640 // 2 * vecs * size * size, bytes_accessed=MIB, transcendentals=0),
    )(table, vec, kept(store), *after)


def kept(store):
    return pltpu.with_memory_space_constraint(store, pltpu.VMEM)


def first_kernel(center, half_width, current, *refs):
    pieces, (out, out_bf) = refs[:-2], refs[-2:]
    image = pieces[0][...]
    for piece in pieces[1:]:
        image += piece[...]
    value = (image - center[0] * current[...]) / half_width[0]
    out[...] = value
    out_bf[...] = value.astype(out_bf.dtype)


def next_kernel(count, center, half_width, current, previous, *refs):
    pieces, outs = refs[:count], refs[count:]
    image = pieces[0][...]
    for piece in pieces[1:]:
        image += piece[...]
    value = 2.0 * (image - center[0] * current[...]) / half_width[0] - previous[...]
    for out in outs:
        out[...] = value.astype(out.dtype)


def on_device(start_vectors, blocks, block_rows, block_cols, live_counts, center, half_width):
    parts = lax.axis_size("col")
    owned = start_vectors.shape[0]
    shape = start_vectors.shape
    scalars = (center.reshape(1), half_width.reshape(1))
    outs = (jax.ShapeDtypeStruct(shape, jnp.float32), jax.ShapeDtypeStruct(shape, jnp.bfloat16))

    def image_pieces(vec):
        pieces, last = [], ()
        for part in (*range(1, parts), 0):
            piece = local_products(part, vec, prep, last, owned, parts)
            last = (piece,)
            if part:
                piece = lax.ppermute(piece, "col", [(i, (i + part) % parts) for i in range(parts)])
            pieces.append(piece)
        return pieces

    start_bf = rounded(start_vectors)
    place, table = sort_plan(block_rows, block_cols, live_counts, scalars, start_bf, parts, owned)
    line = line_gathered(start_bf, (table,), (SMEM,))
    store = prepared(place, table, blocks, line, parts * owned)
    prep = (table, store)
    pieces = image_pieces(all_gathered(line, (kept(store),)))
    first = small_call(first_kernel, outs, [SMEM, SMEM] + [VMEM] * (1 + parts))
    current, current_bf = first(*scalars, start_vectors, *pieces)
    previous = start_vectors
    for turn in range(2):
        pieces = image_pieces(all_gathered(line_gathered(current_bf)))
        wanted = outs[:1] if turn else outs
        step = small_call(functools.partial(next_kernel, parts), wanted, [SMEM, SMEM] + [VMEM] * (2 + parts))
        following, *rest = step(*scalars, current, previous, *pieces)
        previous, current, current_bf = current, following, rest[0] if rest else None
    return current


def solution(mesh):
    return jax.shard_map(
        on_device,
        mesh=mesh,
        in_specs=(
            P(("row", "col"), None, None),
            P(("row", "col"), None, None),
            P(("row", "col")),
            P(("row", "col")),
            P(("row", "col")),
            P(),
            P(),
        ),
        out_specs=P(("row", "col"), None, None),
        check_vma=False,
    )
```

```python
import functools

import jax
import jax.numpy as jnp
from jax import lax
from jax.experimental import pallas as pl
from jax.experimental.pallas import tpu as pltpu
from jax.sharding import PartitionSpec as P


SIDE = 4
CORES = 2
CHUNK = 32
SPARE = 64
GROUP = 4
BATCH = 24
LANES = 256
HEAD = 2 * LANES
PART_ORDER = (2, 1, 3)
MIB = 1 << 20


VMEM = pl.BlockSpec(memory_space=pltpu.VMEM)
SMEM = pl.BlockSpec(memory_space=pltpu.SMEM)


def small_call(kernel, outs, in_specs, flops=1000):
    cost = pl.CostEstimate(flops=flops, bytes_accessed=1000, transcendentals=0)
    return pl.pallas_call(
        kernel,
        out_shape=outs,
        in_specs=in_specs,
        out_specs=jax.tree.map(lambda _: VMEM, outs),
        compiler_params=pltpu.CompilerParams(vmem_limit_bytes=4 * MIB),
        cost_estimate=cost,
    )


def join_kernel(count, *refs):
    parts, out = refs[:count], refs[-1]
    size = parts[0].shape[0]
    for place, part in enumerate(parts):
        out[place * size : (place + 1) * size] = part[...]


def joined(parts, after=(), after_specs=()):
    shape = (len(parts) * parts[0].shape[0], *parts[0].shape[1:])
    kernel = functools.partial(join_kernel, len(parts))
    specs = [VMEM] * len(parts) + list(after_specs or [VMEM] * len(after))
    return small_call(kernel, jax.ShapeDtypeStruct(shape, parts[0].dtype), specs)(*parts, *after)


def round_kernel(value, out):
    out[...] = value[...].astype(out.dtype)


def rounded(value):
    return small_call(round_kernel, jax.ShapeDtypeStruct(value.shape, jnp.bfloat16), [VMEM])(value)


def chip_shifts(dx, dy, dcore=0):
    pairs = []
    for x in range(SIDE):
        for y in range(SIDE):
            for core in range(CORES):
                to = ((x + dx) % SIDE * SIDE + (y + dy) % SIDE) * CORES + (core + dcore) % CORES
                pairs.append(((x * SIDE + y) * CORES + core, to))
    return pairs


def line_gathered(owned, after=(), specs=()):
    return joined([owned] + [lax.ppermute(owned, "row", chip_shifts(0, dy)) for dy in range(1, SIDE)], after, specs)


def all_gathered(line, after=()):
    mine = joined([line] + [lax.ppermute(line, "row", chip_shifts(dx, 0)) for dx in range(1, SIDE)], after)
    theirs = lax.ppermute(mine, "row", chip_shifts(0, 0, 1))
    return joined([mine, theirs])


def padded_room(slots, span):
    step = GROUP * BATCH
    return (slots + span * (GROUP - 1) + step - 1) // step * step


def iota(shape, dim):
    return lax.broadcasted_iota(jnp.int32, shape, dim)


def plan_kernel(parts, owned, live_ref, rows_hbm, cols_hbm, center, half_width, _after, *refs):
    place_out, table_out, center_out, half_out, rows_ref, cols_ref, place_ref, table_ref, sems = refs
    pairs = ((rows_hbm, rows_ref), (cols_hbm, cols_ref))
    fetches = [pltpu.make_async_copy(source, target, sems.at[2 + k]) for k, (source, target) in enumerate(pairs)]
    for fetch in fetches:
        fetch.start()
    center_out[0] = center[...]
    half_out[0] = half_width[...]
    for fetch in fetches:
        fetch.wait()
    live = live_ref[0]
    me, here = lax.axis_index("row"), lax.axis_index("col")
    slots = rows_ref.shape[0]
    rows, cols = rows_ref[...].reshape(1, slots), cols_ref[...].reshape(1, slots)
    span = parts * owned
    lanes = LANES
    head = HEAD
    room = table_ref.shape[1] - head - SPARE

    turned = lax.rem(lax.div(rows, owned) + (parts - here), parts) * owned + lax.rem(rows, owned)
    ids = iota((1, slots), 1)
    alive = ids < live
    hot = jnp.where((turned == iota((span, slots), 0)) & alive, 1.0, 0.0)
    earlier = jnp.where(iota((slots, slots), 0) < iota((slots, slots), 1), 1.0, 0.0).astype(jnp.bfloat16)
    rank = jnp.dot(hot.astype(jnp.bfloat16), earlier, preferred_element_type=jnp.float32)
    counts = jnp.sum(hot, axis=1, keepdims=True).astype(jnp.int32)
    padded = lax.div(counts + (GROUP - 1), GROUP) * GROUP
    row_of, lane_of = iota((span, lanes), 0), iota((span, lanes), 1)
    across = jnp.sum(jnp.where(row_of == lane_of, padded, 0).astype(jnp.float32), axis=0, keepdims=True)
    starts = jnp.sum(jnp.where(lane_of < row_of, across, 0.0), axis=1, keepdims=True)
    ends = starts.astype(jnp.int32) + padded
    place = jnp.sum(hot * (rank + starts), axis=0, keepdims=True).astype(jnp.int32)
    place = jnp.where(alive, place, room + lax.rem(ids, CHUNK))
    place_ref[...] = place

    owner = lax.div(cols, owned)
    chip, my_chip = lax.div(owner, CORES), lax.div(me, CORES)
    dx = lax.rem(lax.div(my_chip, SIDE) + SIDE - lax.div(chip, SIDE), SIDE)
    dy = lax.rem(lax.rem(my_chip, SIDE) + SIDE - lax.rem(chip, SIDE), SIDE)
    dcore = lax.rem(me + owner, CORES)
    source = ((dcore * SIDE + dx) * SIDE + dy) * owned + lax.rem(cols, owned)
    weights = jnp.broadcast_to(jnp.where(alive, source, 0).astype(jnp.float32), (8, slots)).astype(jnp.bfloat16)
    for block in range((room + SPARE) // SPARE):
        match = jnp.where(place == iota((SPARE, slots), 0) + block * SPARE, 1.0, 0.0).astype(jnp.bfloat16)
        found = lax.dot_general(weights, match, (((1,), (1,)), ((), ())), preferred_element_type=jnp.float32)
        table_ref[:, head + block * SPARE : head + (block + 1) * SPARE] = found[:1].astype(jnp.int32)

    ended = jnp.where(ends <= lane_of * GROUP, 1.0, 0.0)
    table_ref[:, lanes:head] = jnp.sum(ended, axis=0, keepdims=True).astype(jnp.int32)
    at_ends = jnp.sum(jnp.where(row_of == lane_of, ends, 0).astype(jnp.float32), axis=0, keepdims=True).astype(jnp.int32)
    lane = iota((1, lanes), 1)
    table_ref[:, :lanes] = jnp.where(lane == span, lax.div(live + (CHUNK - 1), CHUNK), at_ends)
    copies = [
        pltpu.make_async_copy(place_ref, place_out, sems.at[0]),
        pltpu.make_async_copy(table_ref, table_out, sems.at[1]),
    ]
    for copy in copies:
        copy.start()
    for copy in copies:
        copy.wait()


def sort_plan(rows, cols, live, scalars, after, parts, owned):
    slots = rows.shape[0]
    room = padded_room(slots, parts * owned)
    widths = (slots, HEAD + room + SPARE)
    anywhere = pl.BlockSpec(memory_space=pltpu.HBM)
    rows, cols = (pltpu.with_memory_space_constraint(a, pltpu.HBM) for a in (rows, cols))
    return pl.pallas_call(
        functools.partial(plan_kernel, parts, owned),
        out_shape=[pltpu.SMEM((1, width), jnp.int32) for width in widths] + [pltpu.SMEM((1,), jnp.float32)] * 2,
        in_specs=[SMEM, anywhere, anywhere, SMEM, SMEM, VMEM],
        out_specs=[SMEM] * 4,
        scratch_shapes=[pltpu.VMEM((slots,), jnp.int32)] * 2
        + [pltpu.VMEM((1, width), jnp.int32) for width in widths]
        + [pltpu.SemaphoreType.DMA((4,))],
        compiler_params=pltpu.CompilerParams(vmem_limit_bytes=8 * MIB),
        cost_estimate=pl.CostEstimate(flops=1000, bytes_accessed=1000, transcendentals=0),
    )(live, rows, cols, *scalars, after)


def prepare_kernel(span, place, sizes, _after, blocks_hbm, store, raw, sems):
    chunks = sizes[0, span]
    size = raw.shape[1]

    def copy_of(c):
        part = pl.ds(c * CHUNK, CHUNK)
        return pltpu.make_async_copy(blocks_hbm.at[part], raw.at[part], sems.at[c])

    @pl.loop(0, chunks)
    def _(c):
        copy_of(c).start()

    nothing = jnp.zeros((GROUP, size, size), store.dtype)

    @pl.loop(0, span)
    def _(row):
        store[pl.ds(jnp.maximum(sizes[0, row] - GROUP, 0), GROUP)] = nothing

    @pl.loop(0, chunks)
    def _(c):
        copy_of(c).wait()

        for u in range(CHUNK):
            slot = c * CHUNK + u
            store[place[0, slot]] = raw[slot].T


def prepared(place, sizes, blocks, after, span):
    slots, size, _ = blocks.shape
    return pl.pallas_call(
        functools.partial(prepare_kernel, span),
        out_shape=pltpu.VMEM((padded_room(slots, span) + SPARE, size, size), blocks.dtype),
        in_specs=[SMEM] * 2 + [VMEM, pl.BlockSpec(memory_space=pl.ANY)],
        out_specs=VMEM,
        scratch_shapes=[
            pltpu.VMEM((slots, size, size), blocks.dtype),
            pltpu.SemaphoreType.DMA((slots // CHUNK,)),
        ],
        compiler_params=pltpu.CompilerParams(vmem_limit_bytes=24 * MIB),
        cost_estimate=pl.CostEstimate(flops=1000, bytes_accessed=2 * slots * size * size, transcendentals=0),
    )(place, sizes, after, blocks)


def products_kernel(first_row, table, vec, store, *refs):
    out, sums = refs[-2:]
    owned = out.shape[0]
    size = store.shape[1]
    start = lax.div(table[0, first_row - 1], GROUP) if first_row else 0
    count = lax.div(table[0, first_row + owned - 1], GROUP) - start
    sums[...] = jnp.zeros_like(sums)

    @pl.loop(0, lax.div(count + (BATCH - 1), BATCH))
    def _(batch):
        for k in range(BATCH):
            group = start + batch * BATCH + k
            left = jnp.concatenate([vec[table[0, HEAD + group * GROUP + i]] for i in range(GROUP)], axis=1)
            right = store[pl.ds(group * GROUP, GROUP)].reshape(GROUP * size, size)
            sums[table[0, LANES + group]] += jnp.dot(left, right, preferred_element_type=jnp.float32)

    out[...] = sums[first_row : first_row + owned]


def local_products(part, vec, prep, after, owned, parts):
    table, store = prep
    _, vecs, size = vec.shape
    return pl.pallas_call(
        functools.partial(products_kernel, part * owned),
        out_shape=jax.ShapeDtypeStruct((owned, vecs, size), jnp.float32),
        in_specs=[SMEM] + [VMEM] * (2 + len(after)),
        out_specs=VMEM,
        scratch_shapes=[pltpu.VMEM((owned * parts + 1, vecs, size), jnp.float32)],
        compiler_params=pltpu.CompilerParams(vmem_limit_bytes=4 * MIB),
        cost_estimate=pl.CostEstimate(flops=640 // 2 * vecs * size * size, bytes_accessed=MIB, transcendentals=0),
    )(table, vec, kept(store), *after)


def kept(store):
    return pltpu.with_memory_space_constraint(store, pltpu.VMEM)


def first_kernel(center, half_width, current, *refs):
    pieces, (out, out_bf) = refs[:-2], refs[-2:]
    image = pieces[0][...]
    for piece in pieces[1:]:
        image += piece[...]
    value = (image - center[0] * current[...]) / half_width[0]
    out[...] = value
    out_bf[...] = value.astype(out_bf.dtype)


def next_kernel(count, center, half_width, current, previous, *refs):
    pieces, outs = refs[:count], refs[count:]
    image = pieces[0][...]
    for piece in pieces[1:]:
        image += piece[...]
    value = 2.0 * (image - center[0] * current[...]) / half_width[0] - previous[...]
    for out in outs:
        out[...] = value.astype(out.dtype)


def on_device(start_vectors, blocks, block_rows, block_cols, live_counts, center, half_width):
    parts = lax.axis_size("col")
    owned = start_vectors.shape[0]
    shape = start_vectors.shape
    scalars = (center, half_width)
    outs = (jax.ShapeDtypeStruct(shape, jnp.float32), jax.ShapeDtypeStruct(shape, jnp.bfloat16))

    def image_pieces(vec):
        pieces, last = [], ()
        for part in (*PART_ORDER, 0):
            piece = local_products(part, vec, prep, last, owned, parts)
            last = (piece,)
            if part:
                piece = lax.ppermute(piece, "col", [(i, (i + part) % parts) for i in range(parts)])
            pieces.append(piece)
        return pieces

    start_bf = rounded(start_vectors)
    place, table, *scalars = sort_plan(block_rows, block_cols, live_counts, scalars, start_bf, parts, owned)
    line = line_gathered(start_bf, (table,), (SMEM,))
    store = prepared(place, table, blocks, line, parts * owned)
    prep = (table, store)
    pieces = image_pieces(all_gathered(line, (kept(store),)))
    first = small_call(first_kernel, outs, [SMEM, SMEM] + [VMEM] * (1 + parts))
    current, current_bf = first(*scalars, start_vectors, *pieces)
    previous = start_vectors
    for turn in range(2):
        pieces = image_pieces(all_gathered(line_gathered(current_bf)))
        wanted = outs[:1] if turn else outs
        step = small_call(functools.partial(next_kernel, parts), wanted, [SMEM, SMEM] + [VMEM] * (2 + parts))
        following, *rest = step(*scalars, current, previous, *pieces)
        previous, current, current_bf = current, following, rest[0] if rest else None
    return current


def solution(mesh):
    return jax.shard_map(
        on_device,
        mesh=mesh,
        in_specs=(
            P(("row", "col"), None, None),
            P(("row", "col"), None, None),
            P(("row", "col")),
            P(("row", "col")),
            P(("row", "col")),
            P(),
            P(),
        ),
        out_specs=P(("row", "col"), None, None),
        check_vma=False,
    )
```

```python
import functools

import jax
import jax.numpy as jnp
from jax import lax
from jax.experimental import pallas as pl
from jax.experimental.pallas import tpu as pltpu
from jax.sharding import PartitionSpec as P


SIDE = 4
CORES = 2
CHUNK = 32
SPARE = 64
GROUP = 4
BATCH = 24
LANES = 256
HEAD = 2 * LANES
PART_ORDER = (2, 1, 3)
MIB = 1 << 20


VMEM = pl.BlockSpec(memory_space=pltpu.VMEM)
SMEM = pl.BlockSpec(memory_space=pltpu.SMEM)


def small_call(kernel, outs, in_specs, flops=1000):
    cost = pl.CostEstimate(flops=flops, bytes_accessed=1000, transcendentals=0)
    return pl.pallas_call(
        kernel,
        out_shape=outs,
        in_specs=in_specs,
        out_specs=jax.tree.map(lambda _: VMEM, outs),
        compiler_params=pltpu.CompilerParams(vmem_limit_bytes=4 * MIB),
        cost_estimate=cost,
    )


def join_kernel(count, *refs):
    parts, out = refs[:count], refs[-1]
    size = parts[0].shape[0]
    for place, part in enumerate(parts):
        out[place * size : (place + 1) * size] = part[...]


def joined(parts, after=(), after_specs=()):
    shape = (len(parts) * parts[0].shape[0], *parts[0].shape[1:])
    kernel = functools.partial(join_kernel, len(parts))
    specs = [VMEM] * len(parts) + list(after_specs or [VMEM] * len(after))
    return small_call(kernel, jax.ShapeDtypeStruct(shape, parts[0].dtype), specs)(*parts, *after)


def round_kernel(value, out):
    out[...] = value[...].astype(out.dtype)


def rounded(value):
    return small_call(round_kernel, jax.ShapeDtypeStruct(value.shape, jnp.bfloat16), [VMEM])(value)


def chip_shifts(stage, step):
    pairs = []
    for x in range(SIDE):
        for y in range(SIDE):
            for core in range(CORES):
                along_y = stage == core
                to_x = x if along_y else (x + step) % SIDE
                to_y = (y + step) % SIDE if along_y else y
                pairs.append(((x * SIDE + y) * CORES + core, (to_x * SIDE + to_y) * CORES + core))
    return pairs


def core_swap():
    return [(i, i ^ 1) for i in range(SIDE * SIDE * CORES)]


def line_gathered(owned, after=(), specs=()):
    return joined([owned] + [lax.ppermute(owned, "row", chip_shifts(0, step)) for step in range(1, SIDE)], after, specs)


def all_gathered(line, after=()):
    mine = joined([line] + [lax.ppermute(line, "row", chip_shifts(1, step)) for step in range(1, SIDE)], after)
    theirs = lax.ppermute(mine, "row", core_swap())
    return joined([mine, theirs])


def padded_room(slots, span):
    step = GROUP * BATCH
    return (slots + span * (GROUP - 1) + step - 1) // step * step


def iota(shape, dim):
    return lax.broadcasted_iota(jnp.int32, shape, dim)


def plan_kernel(parts, owned, live_ref, rows_hbm, cols_hbm, center, half_width, _after, *refs):
    place_out, table_out, center_out, half_out, rows_ref, cols_ref, place_ref, table_ref, sems = refs
    pairs = ((rows_hbm, rows_ref), (cols_hbm, cols_ref))
    fetches = [pltpu.make_async_copy(source, target, sems.at[2 + k]) for k, (source, target) in enumerate(pairs)]
    for fetch in fetches:
        fetch.start()
    center_out[0] = center[...]
    half_out[0] = half_width[...]
    for fetch in fetches:
        fetch.wait()
    live = live_ref[0]
    me, here = lax.axis_index("row"), lax.axis_index("col")
    slots = rows_ref.shape[0]
    rows, cols = rows_ref[...].reshape(1, slots), cols_ref[...].reshape(1, slots)
    span = parts * owned
    lanes = LANES
    head = HEAD
    room = table_ref.shape[1] - head - SPARE

    turned = lax.rem(lax.div(rows, owned) + (parts - here), parts) * owned + lax.rem(rows, owned)
    ids = iota((1, slots), 1)
    alive = ids < live
    hot = jnp.where((turned == iota((span, slots), 0)) & alive, 1.0, 0.0)
    earlier = jnp.where(iota((slots, slots), 0) < iota((slots, slots), 1), 1.0, 0.0).astype(jnp.bfloat16)
    rank = jnp.dot(hot.astype(jnp.bfloat16), earlier, preferred_element_type=jnp.float32)
    counts = jnp.sum(hot, axis=1, keepdims=True).astype(jnp.int32)
    padded = lax.div(counts + (GROUP - 1), GROUP) * GROUP
    row_of, lane_of = iota((span, lanes), 0), iota((span, lanes), 1)
    across = jnp.sum(jnp.where(row_of == lane_of, padded, 0).astype(jnp.float32), axis=0, keepdims=True)
    starts = jnp.sum(jnp.where(lane_of < row_of, across, 0.0), axis=1, keepdims=True)
    ends = starts.astype(jnp.int32) + padded
    place = jnp.sum(hot * (rank + starts), axis=0, keepdims=True).astype(jnp.int32)
    place = jnp.where(alive, place, room + lax.rem(ids, CHUNK))
    place_ref[...] = place

    owner = lax.div(cols, owned)
    chip, my_chip = lax.div(owner, CORES), lax.div(me, CORES)
    dx = lax.rem(lax.div(my_chip, SIDE) + SIDE - lax.div(chip, SIDE), SIDE)
    dy = lax.rem(lax.rem(my_chip, SIDE) + SIDE - lax.rem(chip, SIDE), SIDE)
    dcore = lax.rem(me + owner, CORES)
    within = jnp.where(lax.rem(owner, CORES) == 0, dx * SIDE + dy, dy * SIDE + dx)
    source = (dcore * (SIDE * SIDE) + within) * owned + lax.rem(cols, owned)
    weights = jnp.broadcast_to(jnp.where(alive, source, 0).astype(jnp.float32), (8, slots)).astype(jnp.bfloat16)
    for block in range((room + SPARE) // SPARE):
        match = jnp.where(place == iota((SPARE, slots), 0) + block * SPARE, 1.0, 0.0).astype(jnp.bfloat16)
        found = lax.dot_general(weights, match, (((1,), (1,)), ((), ())), preferred_element_type=jnp.float32)
        table_ref[:, head + block * SPARE : head + (block + 1) * SPARE] = found[:1].astype(jnp.int32)

    ended = jnp.where(ends <= lane_of * GROUP, 1.0, 0.0)
    table_ref[:, lanes:head] = jnp.sum(ended, axis=0, keepdims=True).astype(jnp.int32)
    at_ends = jnp.sum(jnp.where(row_of == lane_of, ends, 0).astype(jnp.float32), axis=0, keepdims=True).astype(jnp.int32)
    lane = iota((1, lanes), 1)
    table_ref[:, :lanes] = jnp.where(lane == span, lax.div(live + (CHUNK - 1), CHUNK), at_ends)
    copies = [
        pltpu.make_async_copy(place_ref, place_out, sems.at[0]),
        pltpu.make_async_copy(table_ref, table_out, sems.at[1]),
    ]
    for copy in copies:
        copy.start()
    for copy in copies:
        copy.wait()


def sort_plan(rows, cols, live, scalars, after, parts, owned):
    slots = rows.shape[0]
    room = padded_room(slots, parts * owned)
    widths = (slots, HEAD + room + SPARE)
    anywhere = pl.BlockSpec(memory_space=pltpu.HBM)
    rows, cols = (pltpu.with_memory_space_constraint(a, pltpu.HBM) for a in (rows, cols))
    return pl.pallas_call(
        functools.partial(plan_kernel, parts, owned),
        out_shape=[pltpu.SMEM((1, width), jnp.int32) for width in widths] + [pltpu.SMEM((1,), jnp.float32)] * 2,
        in_specs=[SMEM, anywhere, anywhere, SMEM, SMEM, VMEM],
        out_specs=[SMEM] * 4,
        scratch_shapes=[pltpu.VMEM((slots,), jnp.int32)] * 2
        + [pltpu.VMEM((1, width), jnp.int32) for width in widths]
        + [pltpu.SemaphoreType.DMA((4,))],
        compiler_params=pltpu.CompilerParams(vmem_limit_bytes=8 * MIB),
        cost_estimate=pl.CostEstimate(flops=1000, bytes_accessed=1000, transcendentals=0),
    )(live, rows, cols, *scalars, after)


def prepare_kernel(span, place, sizes, _after, blocks_hbm, store, raw, sems):
    chunks = sizes[0, span]
    size = raw.shape[1]

    def copy_of(c):
        part = pl.ds(c * CHUNK, CHUNK)
        return pltpu.make_async_copy(blocks_hbm.at[part], raw.at[part], sems.at[c])

    @pl.loop(0, chunks)
    def _(c):
        copy_of(c).start()

    nothing = jnp.zeros((GROUP, size, size), store.dtype)

    @pl.loop(0, span)
    def _(row):
        store[pl.ds(jnp.maximum(sizes[0, row] - GROUP, 0), GROUP)] = nothing

    @pl.loop(0, chunks)
    def _(c):
        copy_of(c).wait()

        for u in range(CHUNK):
            slot = c * CHUNK + u
            store[place[0, slot]] = raw[slot].T


def prepared(place, sizes, blocks, after, span):
    slots, size, _ = blocks.shape
    return pl.pallas_call(
        functools.partial(prepare_kernel, span),
        out_shape=pltpu.VMEM((padded_room(slots, span) + SPARE, size, size), blocks.dtype),
        in_specs=[SMEM] * 2 + [VMEM, pl.BlockSpec(memory_space=pl.ANY)],
        out_specs=VMEM,
        scratch_shapes=[
            pltpu.VMEM((slots, size, size), blocks.dtype),
            pltpu.SemaphoreType.DMA((slots // CHUNK,)),
        ],
        compiler_params=pltpu.CompilerParams(vmem_limit_bytes=24 * MIB),
        cost_estimate=pl.CostEstimate(flops=1000, bytes_accessed=2 * slots * size * size, transcendentals=0),
    )(place, sizes, after, blocks)


def products_kernel(first_row, table, vec, store, *refs):
    out, sums = refs[-2:]
    owned = out.shape[0]
    size = store.shape[1]
    start = lax.div(table[0, first_row - 1], GROUP) if first_row else 0
    count = lax.div(table[0, first_row + owned - 1], GROUP) - start
    sums[...] = jnp.zeros_like(sums)

    @pl.loop(0, lax.div(count + (BATCH - 1), BATCH))
    def _(batch):
        for k in range(BATCH):
            group = start + batch * BATCH + k
            left = jnp.concatenate([vec[table[0, HEAD + group * GROUP + i]] for i in range(GROUP)], axis=1)
            right = store[pl.ds(group * GROUP, GROUP)].reshape(GROUP * size, size)
            sums[table[0, LANES + group]] += jnp.dot(left, right, preferred_element_type=jnp.float32)

    out[...] = sums[first_row : first_row + owned]


def local_products(part, vec, prep, after, owned, parts):
    table, store = prep
    _, vecs, size = vec.shape
    return pl.pallas_call(
        functools.partial(products_kernel, part * owned),
        out_shape=jax.ShapeDtypeStruct((owned, vecs, size), jnp.float32),
        in_specs=[SMEM] + [VMEM] * (2 + len(after)),
        out_specs=VMEM,
        scratch_shapes=[pltpu.VMEM((owned * parts + 1, vecs, size), jnp.float32)],
        compiler_params=pltpu.CompilerParams(vmem_limit_bytes=4 * MIB),
        cost_estimate=pl.CostEstimate(flops=640 // 2 * vecs * size * size, bytes_accessed=MIB, transcendentals=0),
    )(table, vec, kept(store), *after)


def kept(store):
    return pltpu.with_memory_space_constraint(store, pltpu.VMEM)


def first_kernel(center, half_width, current, *refs):
    pieces, (out, out_bf) = refs[:-2], refs[-2:]
    image = pieces[0][...]
    for piece in pieces[1:]:
        image += piece[...]
    value = (image - center[0] * current[...]) / half_width[0]
    out[...] = value
    out_bf[...] = value.astype(out_bf.dtype)


def next_kernel(count, center, half_width, current, previous, *refs):
    pieces, outs = refs[:count], refs[count:]
    image = pieces[0][...]
    for piece in pieces[1:]:
        image += piece[...]
    value = 2.0 * (image - center[0] * current[...]) / half_width[0] - previous[...]
    for out in outs:
        out[...] = value.astype(out.dtype)


def on_device(start_vectors, blocks, block_rows, block_cols, live_counts, center, half_width):
    parts = lax.axis_size("col")
    owned = start_vectors.shape[0]
    shape = start_vectors.shape
    scalars = (center, half_width)
    outs = (jax.ShapeDtypeStruct(shape, jnp.float32), jax.ShapeDtypeStruct(shape, jnp.bfloat16))

    def image_pieces(vec):
        pieces, last = [], ()
        for part in (*PART_ORDER, 0):
            piece = local_products(part, vec, prep, last, owned, parts)
            last = (piece,)
            if part:
                piece = lax.ppermute(piece, "col", [(i, (i + part) % parts) for i in range(parts)])
            pieces.append(piece)
        return pieces

    start_bf = rounded(start_vectors)
    place, table, *scalars = sort_plan(block_rows, block_cols, live_counts, scalars, start_bf, parts, owned)
    line = line_gathered(start_bf, (table,), (SMEM,))
    store = prepared(place, table, blocks, line, parts * owned)
    prep = (table, store)
    pieces = image_pieces(all_gathered(line, (kept(store),)))
    first = small_call(first_kernel, outs, [SMEM, SMEM] + [VMEM] * (1 + parts))
    current, current_bf = first(*scalars, start_vectors, *pieces)
    previous = start_vectors
    for turn in range(2):
        pieces = image_pieces(all_gathered(line_gathered(current_bf)))
        wanted = outs[:1] if turn else outs
        step = small_call(functools.partial(next_kernel, parts), wanted, [SMEM, SMEM] + [VMEM] * (2 + parts))
        following, *rest = step(*scalars, current, previous, *pieces)
        previous, current, current_bf = current, following, rest[0] if rest else None
    return current


def solution(mesh):
    return jax.shard_map(
        on_device,
        mesh=mesh,
        in_specs=(
            P(("row", "col"), None, None),
            P(("row", "col"), None, None),
            P(("row", "col")),
            P(("row", "col")),
            P(("row", "col")),
            P(),
            P(),
        ),
        out_specs=P(("row", "col"), None, None),
        check_vma=False,
    )
```

```python
import functools

import jax
import jax.numpy as jnp
from jax import lax
from jax.experimental import pallas as pl
from jax.experimental.pallas import tpu as pltpu
from jax.sharding import PartitionSpec as P


SIDE = 4
CORES = 2
CHUNK = 32
SPARE = 64
GROUP = 4
BATCH = 24
LANES = 256
HEAD = 2 * LANES
PART_ORDER = (2, 1, 3)
STEP_ORDER = (1, 3, 2)
MIB = 1 << 20


VMEM = pl.BlockSpec(memory_space=pltpu.VMEM)
SMEM = pl.BlockSpec(memory_space=pltpu.SMEM)


def small_call(kernel, outs, in_specs, flops=1000):
    cost = pl.CostEstimate(flops=flops, bytes_accessed=1000, transcendentals=0)
    return pl.pallas_call(
        kernel,
        out_shape=outs,
        in_specs=in_specs,
        out_specs=jax.tree.map(lambda _: VMEM, outs),
        compiler_params=pltpu.CompilerParams(vmem_limit_bytes=4 * MIB),
        cost_estimate=cost,
    )


def join_kernel(places, *refs):
    parts, out = refs[: len(places)], refs[-1]
    size = parts[0].shape[0]
    for place, part in zip(places, parts):
        out[place * size : (place + 1) * size] = part[...]


def joined(parts, after=(), after_specs=(), places=(0, 1)):
    shape = (len(parts) * parts[0].shape[0], *parts[0].shape[1:])
    kernel = functools.partial(join_kernel, places)
    specs = [VMEM] * len(parts) + list(after_specs or [VMEM] * len(after))
    return small_call(kernel, jax.ShapeDtypeStruct(shape, parts[0].dtype), specs)(*parts, *after)


def round_kernel(value, out):
    out[...] = value[...].astype(out.dtype)


def rounded(value):
    return small_call(round_kernel, jax.ShapeDtypeStruct(value.shape, jnp.bfloat16), [VMEM])(value)


def chip_shifts(stage, step):
    pairs = []
    for x in range(SIDE):
        for y in range(SIDE):
            for core in range(CORES):
                along_y = stage == core
                to_x = x if along_y else (x + step) % SIDE
                to_y = (y + step) % SIDE if along_y else y
                pairs.append(((x * SIDE + y) * CORES + core, (to_x * SIDE + to_y) * CORES + core))
    return pairs


def core_swap():
    return [(i, i ^ 1) for i in range(SIDE * SIDE * CORES)]


def shifted(value, stage):
    return [value] + [lax.ppermute(value, "row", chip_shifts(stage, step)) for step in STEP_ORDER]


def line_gathered(owned, after=(), specs=()):
    return joined(shifted(owned, 0), after, specs, (0, *STEP_ORDER))


def all_gathered(line, after=()):
    mine = joined(shifted(line, 1), after, (), (0, *STEP_ORDER))
    return joined([mine, lax.ppermute(mine, "row", core_swap())])


def padded_room(slots, span):
    step = GROUP * BATCH
    return (slots + span * (GROUP - 1) + step - 1) // step * step


def iota(shape, dim):
    return lax.broadcasted_iota(jnp.int32, shape, dim)


def plan_kernel(parts, owned, live_ref, rows_hbm, cols_hbm, center, half_width, _after, *refs):
    place_out, table_out, center_out, half_out, rows_ref, cols_ref, place_ref, table_ref, sems = refs
    pairs = ((rows_hbm, rows_ref), (cols_hbm, cols_ref))
    fetches = [pltpu.make_async_copy(source, target, sems.at[2 + k]) for k, (source, target) in enumerate(pairs)]
    for fetch in fetches:
        fetch.start()
    center_out[0] = center[...]
    half_out[0] = half_width[...]
    for fetch in fetches:
        fetch.wait()
    live = live_ref[0]
    me, here = lax.axis_index("row"), lax.axis_index("col")
    slots = rows_ref.shape[0]
    rows, cols = rows_ref[...].reshape(1, slots), cols_ref[...].reshape(1, slots)
    span = parts * owned
    lanes = LANES
    head = HEAD
    room = table_ref.shape[1] - head - SPARE

    turned = lax.rem(lax.div(rows, owned) + (parts - here), parts) * owned + lax.rem(rows, owned)
    ids = iota((1, slots), 1)
    alive = ids < live
    hot = jnp.where((turned == iota((span, slots), 0)) & alive, 1.0, 0.0)
    earlier = jnp.where(iota((slots, slots), 0) < iota((slots, slots), 1), 1.0, 0.0).astype(jnp.bfloat16)
    rank = jnp.dot(hot.astype(jnp.bfloat16), earlier, preferred_element_type=jnp.float32)
    counts = jnp.sum(hot, axis=1, keepdims=True).astype(jnp.int32)
    padded = lax.div(counts + (GROUP - 1), GROUP) * GROUP
    row_of, lane_of = iota((span, lanes), 0), iota((span, lanes), 1)
    across = jnp.sum(jnp.where(row_of == lane_of, padded, 0).astype(jnp.float32), axis=0, keepdims=True)
    starts = jnp.sum(jnp.where(lane_of < row_of, across, 0.0), axis=1, keepdims=True)
    ends = starts.astype(jnp.int32) + padded
    place = jnp.sum(hot * (rank + starts), axis=0, keepdims=True).astype(jnp.int32)
    place = jnp.where(alive, place, room + lax.rem(ids, CHUNK))
    place_ref[...] = place

    owner = lax.div(cols, owned)
    chip, my_chip = lax.div(owner, CORES), lax.div(me, CORES)
    dx = lax.rem(lax.div(my_chip, SIDE) + SIDE - lax.div(chip, SIDE), SIDE)
    dy = lax.rem(lax.rem(my_chip, SIDE) + SIDE - lax.rem(chip, SIDE), SIDE)
    dcore = lax.rem(me + owner, CORES)
    within = jnp.where(lax.rem(owner, CORES) == 0, dx * SIDE + dy, dy * SIDE + dx)
    source = (dcore * (SIDE * SIDE) + within) * owned + lax.rem(cols, owned)
    weights = jnp.broadcast_to(jnp.where(alive, source, 0).astype(jnp.float32), (8, slots)).astype(jnp.bfloat16)
    for block in range((room + SPARE) // SPARE):
        match = jnp.where(place == iota((SPARE, slots), 0) + block * SPARE, 1.0, 0.0).astype(jnp.bfloat16)
        found = lax.dot_general(weights, match, (((1,), (1,)), ((), ())), preferred_element_type=jnp.float32)
        table_ref[:, head + block * SPARE : head + (block + 1) * SPARE] = found[:1].astype(jnp.int32)

    ended = jnp.where(ends <= lane_of * GROUP, 1.0, 0.0)
    table_ref[:, lanes:head] = jnp.sum(ended, axis=0, keepdims=True).astype(jnp.int32)
    at_ends = jnp.sum(jnp.where(row_of == lane_of, ends, 0).astype(jnp.float32), axis=0, keepdims=True).astype(jnp.int32)
    lane = iota((1, lanes), 1)
    table_ref[:, :lanes] = jnp.where(lane == span, lax.div(live + (CHUNK - 1), CHUNK), at_ends)
    copies = [
        pltpu.make_async_copy(place_ref, place_out, sems.at[0]),
        pltpu.make_async_copy(table_ref, table_out, sems.at[1]),
    ]
    for copy in copies:
        copy.start()
    for copy in copies:
        copy.wait()


def sort_plan(rows, cols, live, scalars, after, parts, owned):
    slots = rows.shape[0]
    room = padded_room(slots, parts * owned)
    widths = (slots, HEAD + room + SPARE)
    anywhere = pl.BlockSpec(memory_space=pltpu.HBM)
    rows, cols = (pltpu.with_memory_space_constraint(a, pltpu.HBM) for a in (rows, cols))
    return pl.pallas_call(
        functools.partial(plan_kernel, parts, owned),
        out_shape=[pltpu.SMEM((1, width), jnp.int32) for width in widths] + [pltpu.SMEM((1,), jnp.float32)] * 2,
        in_specs=[SMEM, anywhere, anywhere, SMEM, SMEM, VMEM],
        out_specs=[SMEM] * 4,
        scratch_shapes=[pltpu.VMEM((slots,), jnp.int32)] * 2
        + [pltpu.VMEM((1, width), jnp.int32) for width in widths]
        + [pltpu.SemaphoreType.DMA((4,))],
        compiler_params=pltpu.CompilerParams(vmem_limit_bytes=8 * MIB),
        cost_estimate=pl.CostEstimate(flops=1000, bytes_accessed=1000, transcendentals=0),
    )(live, rows, cols, *scalars, after)


def prepare_kernel(span, place, sizes, _after, blocks_hbm, store, raw, sems):
    chunks = sizes[0, span]
    size = raw.shape[1]

    def copy_of(c):
        part = pl.ds(c * CHUNK, CHUNK)
        return pltpu.make_async_copy(blocks_hbm.at[part], raw.at[part], sems.at[c])

    @pl.loop(0, chunks)
    def _(c):
        copy_of(c).start()

    nothing = jnp.zeros((GROUP, size, size), store.dtype)

    @pl.loop(0, span)
    def _(row):
        store[pl.ds(jnp.maximum(sizes[0, row] - GROUP, 0), GROUP)] = nothing

    @pl.loop(0, chunks)
    def _(c):
        copy_of(c).wait()

        for u in range(CHUNK):
            slot = c * CHUNK + u
            store[place[0, slot]] = raw[slot].T


def prepared(place, sizes, blocks, after, span):
    slots, size, _ = blocks.shape
    return pl.pallas_call(
        functools.partial(prepare_kernel, span),
        out_shape=pltpu.VMEM((padded_room(slots, span) + SPARE, size, size), blocks.dtype),
        in_specs=[SMEM] * 2 + [VMEM, pl.BlockSpec(memory_space=pl.ANY)],
        out_specs=VMEM,
        scratch_shapes=[
            pltpu.VMEM((slots, size, size), blocks.dtype),
            pltpu.SemaphoreType.DMA((slots // CHUNK,)),
        ],
        compiler_params=pltpu.CompilerParams(vmem_limit_bytes=24 * MIB),
        cost_estimate=pl.CostEstimate(flops=1000, bytes_accessed=2 * slots * size * size, transcendentals=0),
    )(place, sizes, after, blocks)


def products_kernel(first_row, table, vec, store, *refs):
    out, sums = refs[-2:]
    owned = out.shape[0]
    size = store.shape[1]
    start = lax.div(table[0, first_row - 1], GROUP) if first_row else 0
    count = lax.div(table[0, first_row + owned - 1], GROUP) - start
    sums[...] = jnp.zeros_like(sums)

    @pl.loop(0, lax.div(count + (BATCH - 1), BATCH))
    def _(batch):
        for k in range(BATCH):
            group = start + batch * BATCH + k
            left = jnp.concatenate([vec[table[0, HEAD + group * GROUP + i]] for i in range(GROUP)], axis=1)
            right = store[pl.ds(group * GROUP, GROUP)].reshape(GROUP * size, size)
            sums[table[0, LANES + group]] += jnp.dot(left, right, preferred_element_type=jnp.float32)

    out[...] = sums[first_row : first_row + owned]


def local_products(part, vec, prep, after, owned, parts):
    table, store = prep
    _, vecs, size = vec.shape
    return pl.pallas_call(
        functools.partial(products_kernel, part * owned),
        out_shape=jax.ShapeDtypeStruct((owned, vecs, size), jnp.float32),
        in_specs=[SMEM] + [VMEM] * (2 + len(after)),
        out_specs=VMEM,
        scratch_shapes=[pltpu.VMEM((owned * parts + 1, vecs, size), jnp.float32)],
        compiler_params=pltpu.CompilerParams(vmem_limit_bytes=4 * MIB),
        cost_estimate=pl.CostEstimate(flops=640 // 2 * vecs * size * size, bytes_accessed=MIB, transcendentals=0),
    )(table, vec, kept(store), *after)


def kept(store):
    return pltpu.with_memory_space_constraint(store, pltpu.VMEM)


def first_kernel(center, half_width, current, *refs):
    pieces, (out, out_bf) = refs[:-2], refs[-2:]
    image = pieces[0][...]
    for piece in pieces[1:]:
        image += piece[...]
    value = (image - center[0] * current[...]) / half_width[0]
    out[...] = value
    out_bf[...] = value.astype(out_bf.dtype)


def next_kernel(count, center, half_width, current, previous, *refs):
    pieces, outs = refs[:count], refs[count:]
    image = pieces[0][...]
    for piece in pieces[1:]:
        image += piece[...]
    value = 2.0 * (image - center[0] * current[...]) / half_width[0] - previous[...]
    for out in outs:
        out[...] = value.astype(out.dtype)


def on_device(start_vectors, blocks, block_rows, block_cols, live_counts, center, half_width):
    parts = lax.axis_size("col")
    owned = start_vectors.shape[0]
    shape = start_vectors.shape
    scalars = (center, half_width)
    outs = (jax.ShapeDtypeStruct(shape, jnp.float32), jax.ShapeDtypeStruct(shape, jnp.bfloat16))

    def image_pieces(vec):
        pieces, last = [], ()
        for part in (*PART_ORDER, 0):
            piece = local_products(part, vec, prep, last, owned, parts)
            last = (piece,)
            if part:
                piece = lax.ppermute(piece, "col", [(i, (i + part) % parts) for i in range(parts)])
            pieces.append(piece)
        return pieces

    start_bf = rounded(start_vectors)
    place, table, *scalars = sort_plan(block_rows, block_cols, live_counts, scalars, start_bf, parts, owned)
    line = line_gathered(start_bf, (table,), (SMEM,))
    store = prepared(place, table, blocks, line, parts * owned)
    prep = (table, store)
    pieces = image_pieces(all_gathered(line, (kept(store),)))
    first = small_call(first_kernel, outs, [SMEM, SMEM] + [VMEM] * (1 + parts))
    current, current_bf = first(*scalars, start_vectors, *pieces)
    previous = start_vectors
    for turn in range(2):
        pieces = image_pieces(all_gathered(line_gathered(current_bf)))
        wanted = outs[:1] if turn else outs
        step = small_call(functools.partial(next_kernel, parts), wanted, [SMEM, SMEM] + [VMEM] * (2 + parts))
        following, *rest = step(*scalars, current, previous, *pieces)
        previous, current, current_bf = current, following, rest[0] if rest else None
    return current


def solution(mesh):
    return jax.shard_map(
        on_device,
        mesh=mesh,
        in_specs=(
            P(("row", "col"), None, None),
            P(("row", "col"), None, None),
            P(("row", "col")),
            P(("row", "col")),
            P(("row", "col")),
            P(),
            P(),
        ),
        out_specs=P(("row", "col"), None, None),
        check_vma=False,
    )
```

```python
import functools

import jax
import jax.numpy as jnp
from jax import lax
from jax.experimental import pallas as pl
from jax.experimental.pallas import tpu as pltpu
from jax.sharding import PartitionSpec as P


SIDE = 4
CORES = 2
CHUNK = 32
SPARE = 64
GROUP = 4
BATCH = 24
LANES = 256
HEAD = 2 * LANES
PART_ORDER = (2, 1, 3)
STEP_ORDER = (1, 3, 2)
MIB = 1 << 20


VMEM = pl.BlockSpec(memory_space=pltpu.VMEM)
SMEM = pl.BlockSpec(memory_space=pltpu.SMEM)


def small_call(kernel, outs, in_specs, flops=1000):
    cost = pl.CostEstimate(flops=flops, bytes_accessed=1000, transcendentals=0)
    return pl.pallas_call(
        kernel,
        out_shape=outs,
        in_specs=in_specs,
        out_specs=jax.tree.map(lambda _: VMEM, outs),
        compiler_params=pltpu.CompilerParams(vmem_limit_bytes=4 * MIB),
        cost_estimate=cost,
    )


def join_kernel(places, *refs):
    parts, out = refs[: len(places)], refs[-1]
    size = parts[0].shape[0]
    for place, part in zip(places, parts):
        out[place * size : (place + 1) * size] = part[...]


def joined(parts, after=(), after_specs=(), places=(0, 1)):
    shape = (len(parts) * parts[0].shape[0], *parts[0].shape[1:])
    kernel = functools.partial(join_kernel, places)
    specs = [VMEM] * len(parts) + list(after_specs or [VMEM] * len(after))
    return small_call(kernel, jax.ShapeDtypeStruct(shape, parts[0].dtype), specs)(*parts, *after)


def round_kernel(value, out):
    out[...] = value[...].astype(out.dtype)


def rounded(value):
    return small_call(round_kernel, jax.ShapeDtypeStruct(value.shape, jnp.bfloat16), [VMEM])(value)


def chip_shifts(stage, step):
    pairs = []
    for x in range(SIDE):
        for y in range(SIDE):
            for core in range(CORES):
                along_y = stage == core
                to_x = x if along_y else (x + step) % SIDE
                to_y = (y + step) % SIDE if along_y else y
                pairs.append(((x * SIDE + y) * CORES + core, (to_x * SIDE + to_y) * CORES + core))
    return pairs


def core_swap():
    return [(i, i ^ 1) for i in range(SIDE * SIDE * CORES)]


def shifted(value, stage):
    return [value] + [lax.ppermute(value, "row", chip_shifts(stage, step)) for step in STEP_ORDER]


def line_gathered(owned, after=(), specs=()):
    return joined(shifted(owned, 0), after, specs, (0, *STEP_ORDER))


def all_gathered(line, after=()):
    mine = joined(shifted(line, 1), after, (), (0, *STEP_ORDER))
    return joined([mine, lax.ppermute(mine, "row", core_swap())])


def padded_room(slots, span):
    step = GROUP * BATCH
    return (slots + span * (GROUP - 1) + step - 1) // step * step


def iota(shape, dim):
    return lax.broadcasted_iota(jnp.int32, shape, dim)


def plan_kernel(parts, owned, live_ref, rows_hbm, cols_hbm, center, half_width, _after, *refs):
    place_out, table_out, center_out, half_out, rows_ref, cols_ref, place_ref, table_ref, sems = refs
    pairs = ((rows_hbm, rows_ref), (cols_hbm, cols_ref))
    fetches = [pltpu.make_async_copy(source, target, sems.at[2 + k]) for k, (source, target) in enumerate(pairs)]
    for fetch in fetches:
        fetch.start()
    center_out[0] = center[...]
    half_out[0] = half_width[...]
    for fetch in fetches:
        fetch.wait()
    live = live_ref[0]
    me, here = lax.axis_index("row"), lax.axis_index("col")
    slots = rows_ref.shape[0]
    rows, cols = rows_ref[...].reshape(1, slots), cols_ref[...].reshape(1, slots)
    span = parts * owned
    lanes = LANES
    head = HEAD
    room = table_ref.shape[1] - head - SPARE

    turned = lax.rem(lax.div(rows, owned) + (parts - here), parts) * owned + lax.rem(rows, owned)
    ids = iota((1, slots), 1)
    alive = ids < live
    hot = jnp.where((turned == iota((span, slots), 0)) & alive, 1.0, 0.0)
    earlier = jnp.where(iota((slots, slots), 0) < iota((slots, slots), 1), 1.0, 0.0).astype(jnp.bfloat16)
    rank = jnp.dot(hot.astype(jnp.bfloat16), earlier, preferred_element_type=jnp.float32)
    counts = jnp.sum(hot, axis=1, keepdims=True).astype(jnp.int32)
    padded = lax.div(counts + (GROUP - 1), GROUP) * GROUP
    row_of, lane_of = iota((span, lanes), 0), iota((span, lanes), 1)
    across = jnp.sum(jnp.where(row_of == lane_of, padded, 0).astype(jnp.float32), axis=0, keepdims=True)
    starts = jnp.sum(jnp.where(lane_of < row_of, across, 0.0), axis=1, keepdims=True)
    ends = starts.astype(jnp.int32) + padded
    place = jnp.sum(hot * (rank + starts), axis=0, keepdims=True).astype(jnp.int32)
    place = jnp.where(alive, place, room + lax.rem(ids, CHUNK))
    place_ref[...] = place

    owner = lax.div(cols, owned)
    chip, my_chip = lax.div(owner, CORES), lax.div(me, CORES)
    dx = lax.rem(lax.div(my_chip, SIDE) + SIDE - lax.div(chip, SIDE), SIDE)
    dy = lax.rem(lax.rem(my_chip, SIDE) + SIDE - lax.rem(chip, SIDE), SIDE)
    dcore = lax.rem(me + owner, CORES)
    within = jnp.where(lax.rem(owner, CORES) == 0, dx * SIDE + dy, dy * SIDE + dx)
    source = (dcore * (SIDE * SIDE) + within) * owned + lax.rem(cols, owned)
    weights = jnp.broadcast_to(jnp.where(alive, source, 0).astype(jnp.float32), (8, slots)).astype(jnp.bfloat16)
    for block in range((room + SPARE) // SPARE):
        match = jnp.where(place == iota((SPARE, slots), 0) + block * SPARE, 1.0, 0.0).astype(jnp.bfloat16)
        found = lax.dot_general(weights, match, (((1,), (1,)), ((), ())), preferred_element_type=jnp.float32)
        table_ref[:, head + block * SPARE : head + (block + 1) * SPARE] = found[:1].astype(jnp.int32)

    ended = jnp.where(ends <= lane_of * GROUP, 1.0, 0.0)
    table_ref[:, lanes:head] = jnp.sum(ended, axis=0, keepdims=True).astype(jnp.int32)
    at_ends = jnp.sum(jnp.where(row_of == lane_of, ends, 0).astype(jnp.float32), axis=0, keepdims=True).astype(jnp.int32)
    lane = iota((1, lanes), 1)
    table_ref[:, :lanes] = jnp.where(lane == span, lax.div(live + (CHUNK - 1), CHUNK), at_ends)
    copies = [
        pltpu.make_async_copy(place_ref, place_out, sems.at[0]),
        pltpu.make_async_copy(table_ref, table_out, sems.at[1]),
    ]
    for copy in copies:
        copy.start()
    for copy in copies:
        copy.wait()


def sort_plan(rows, cols, live, scalars, after, parts, owned):
    slots = rows.shape[0]
    room = padded_room(slots, parts * owned)
    widths = (slots, HEAD + room + SPARE)
    anywhere = pl.BlockSpec(memory_space=pltpu.HBM)
    rows, cols = (pltpu.with_memory_space_constraint(a, pltpu.HBM) for a in (rows, cols))
    return pl.pallas_call(
        functools.partial(plan_kernel, parts, owned),
        out_shape=[pltpu.SMEM((1, width), jnp.int32) for width in widths] + [pltpu.SMEM((1,), jnp.float32)] * 2,
        in_specs=[SMEM, anywhere, anywhere, SMEM, SMEM, VMEM],
        out_specs=[SMEM] * 4,
        scratch_shapes=[pltpu.VMEM((slots,), jnp.int32)] * 2
        + [pltpu.VMEM((1, width), jnp.int32) for width in widths]
        + [pltpu.SemaphoreType.DMA((4,))],
        compiler_params=pltpu.CompilerParams(vmem_limit_bytes=8 * MIB),
        cost_estimate=pl.CostEstimate(flops=1000, bytes_accessed=1000, transcendentals=0),
    )(live, rows, cols, *scalars, after)


def prepare_kernel(span, place, sizes, _after, blocks_hbm, store, raw, sems):
    chunks = sizes[0, span]
    size = raw.shape[1]

    def copy_of(c):
        part = pl.ds(c * CHUNK, CHUNK)
        return pltpu.make_async_copy(blocks_hbm.at[part], raw.at[part], sems.at[c])

    @pl.loop(0, chunks)
    def _(c):
        copy_of(c).start()

    nothing = jnp.zeros((GROUP, size, size), store.dtype)

    @pl.loop(0, span)
    def _(row):
        store[pl.ds(jnp.maximum(sizes[0, row] - GROUP, 0), GROUP)] = nothing

    @pl.loop(0, chunks)
    def _(c):
        copy_of(c).wait()

        for u in range(CHUNK):
            slot = c * CHUNK + u
            store[place[0, slot]] = raw[slot].T


def prepared(place, sizes, blocks, after, span):
    slots, size, _ = blocks.shape
    return pl.pallas_call(
        functools.partial(prepare_kernel, span),
        out_shape=pltpu.VMEM((padded_room(slots, span) + SPARE, size, size), blocks.dtype),
        in_specs=[SMEM] * 2 + [VMEM, pl.BlockSpec(memory_space=pl.ANY)],
        out_specs=VMEM,
        scratch_shapes=[
            pltpu.VMEM((slots, size, size), blocks.dtype),
            pltpu.SemaphoreType.DMA((slots // CHUNK,)),
        ],
        compiler_params=pltpu.CompilerParams(vmem_limit_bytes=24 * MIB),
        cost_estimate=pl.CostEstimate(flops=1000, bytes_accessed=2 * slots * size * size, transcendentals=0),
    )(place, sizes, after, blocks)


def products_kernel(first_row, table, vec, store, *refs):
    out, sums = refs[-2:]
    owned = out.shape[0]
    size = store.shape[1]
    start = lax.div(table[0, first_row - 1], GROUP) if first_row else 0
    count = lax.div(table[0, first_row + owned - 1], GROUP) - start
    sums[...] = jnp.zeros_like(sums)

    @pl.loop(0, lax.div(count + (BATCH - 1), BATCH))
    def _(batch):
        for k in range(BATCH):
            group = start + batch * BATCH + k
            left = jnp.concatenate([vec[table[0, HEAD + group * GROUP + i]] for i in range(GROUP)], axis=1)
            right = store[pl.ds(group * GROUP, GROUP)].reshape(GROUP * size, size)
            sums[table[0, LANES + group]] += jnp.dot(left, right, preferred_element_type=jnp.float32)

    out[...] = sums[first_row : first_row + owned].astype(out.dtype)


def local_products(part, vec, prep, after, owned, parts):
    table, store = prep
    _, vecs, size = vec.shape
    return pl.pallas_call(
        functools.partial(products_kernel, part * owned),
        out_shape=jax.ShapeDtypeStruct((owned, vecs, size), jnp.bfloat16 if part else jnp.float32),
        in_specs=[SMEM] + [VMEM] * (2 + len(after)),
        out_specs=VMEM,
        scratch_shapes=[pltpu.VMEM((owned * parts + 1, vecs, size), jnp.float32)],
        compiler_params=pltpu.CompilerParams(vmem_limit_bytes=4 * MIB),
        cost_estimate=pl.CostEstimate(flops=640 // 2 * vecs * size * size, bytes_accessed=MIB, transcendentals=0),
    )(table, vec, kept(store), *after)


def kept(store):
    return pltpu.with_memory_space_constraint(store, pltpu.VMEM)


def first_kernel(center, half_width, current, *refs):
    pieces, (out, out_bf) = refs[:-2], refs[-2:]
    image = pieces[0][...]
    for piece in pieces[1:]:
        image += piece[...].astype(jnp.float32)
    value = (image - center[0] * current[...]) / half_width[0]
    out[...] = value
    out_bf[...] = value.astype(out_bf.dtype)


def next_kernel(count, center, half_width, current, previous, *refs):
    pieces, outs = refs[:count], refs[count:]
    image = pieces[0][...]
    for piece in pieces[1:]:
        image += piece[...].astype(jnp.float32)
    value = 2.0 * (image - center[0] * current[...]) / half_width[0] - previous[...]
    for out in outs:
        out[...] = value.astype(out.dtype)


def on_device(start_vectors, blocks, block_rows, block_cols, live_counts, center, half_width):
    parts = lax.axis_size("col")
    owned = start_vectors.shape[0]
    shape = start_vectors.shape
    scalars = (center, half_width)
    outs = (jax.ShapeDtypeStruct(shape, jnp.float32), jax.ShapeDtypeStruct(shape, jnp.bfloat16))

    def image_pieces(vec):
        pieces, last = [], ()
        for part in (*PART_ORDER, 0):
            piece = local_products(part, vec, prep, last, owned, parts)
            last = (piece,)
            if part:
                piece = lax.ppermute(piece, "col", [(i, (i + part) % parts) for i in range(parts)])
            pieces.append(piece)
        return pieces

    start_bf = rounded(start_vectors)
    place, table, *scalars = sort_plan(block_rows, block_cols, live_counts, scalars, start_bf, parts, owned)
    line = line_gathered(start_bf, (table,), (SMEM,))
    store = prepared(place, table, blocks, line, parts * owned)
    prep = (table, store)
    pieces = image_pieces(all_gathered(line, (kept(store),)))
    first = small_call(first_kernel, outs, [SMEM, SMEM] + [VMEM] * (1 + parts))
    current, current_bf = first(*scalars, start_vectors, *pieces)
    previous = start_vectors
    for turn in range(2):
        pieces = image_pieces(all_gathered(line_gathered(current_bf)))
        wanted = outs[:1] if turn else outs
        step = small_call(functools.partial(next_kernel, parts), wanted, [SMEM, SMEM] + [VMEM] * (2 + parts))
        following, *rest = step(*scalars, current, previous, *pieces)
        previous, current, current_bf = current, following, rest[0] if rest else None
    return current


def solution(mesh):
    return jax.shard_map(
        on_device,
        mesh=mesh,
        in_specs=(
            P(("row", "col"), None, None),
            P(("row", "col"), None, None),
            P(("row", "col")),
            P(("row", "col")),
            P(("row", "col")),
            P(),
            P(),
        ),
        out_specs=P(("row", "col"), None, None),
        check_vma=False,
    )
```

```python
import functools

import jax
import jax.numpy as jnp
from jax import lax
from jax.experimental import pallas as pl
from jax.experimental.pallas import tpu as pltpu
from jax.sharding import PartitionSpec as P


SIDE = 4
CORES = 2
CHUNK = 32
SPARE = 64
GROUP = 4
BATCH = 24
LANES = 256
HEAD = 2 * LANES
PART_ORDER = (2, 1, 3)
STEP_ORDER = (1, 3, 2)
MIB = 1 << 20


VMEM = pl.BlockSpec(memory_space=pltpu.VMEM)
SMEM = pl.BlockSpec(memory_space=pltpu.SMEM)


def small_call(kernel, outs, in_specs, flops=1000):
    cost = pl.CostEstimate(flops=flops, bytes_accessed=1000, transcendentals=0)
    return pl.pallas_call(
        kernel,
        out_shape=outs,
        in_specs=in_specs,
        out_specs=jax.tree.map(lambda _: VMEM, outs),
        compiler_params=pltpu.CompilerParams(vmem_limit_bytes=4 * MIB),
        cost_estimate=cost,
    )


def join_kernel(starts, *refs):
    out = refs[-1]
    for start, part in zip(starts, refs):
        out[start : start + part.shape[0]] = part[...]


def joined(parts, after=(), after_specs=(), places=None):
    starts = [sum(part.shape[0] for part in parts[:k]) for k in range(len(parts))]
    if places:
        starts = [place * parts[0].shape[0] for place in places]
    shape = (sum(part.shape[0] for part in parts), *parts[0].shape[1:])
    kernel = functools.partial(join_kernel, starts)
    specs = [VMEM] * len(parts) + list(after_specs or [VMEM] * len(after))
    return small_call(kernel, jax.ShapeDtypeStruct(shape, parts[0].dtype), specs)(*parts, *after)


def round_kernel(value, out):
    out[...] = value[...].astype(out.dtype)


def rounded(value):
    return small_call(round_kernel, jax.ShapeDtypeStruct(value.shape, jnp.bfloat16), [VMEM])(value)


def chip_shifts(stage, step):
    pairs = []
    for x in range(SIDE):
        for y in range(SIDE):
            for core in range(CORES):
                along_y = stage == core
                to_x = x if along_y else (x + step) % SIDE
                to_y = (y + step) % SIDE if along_y else y
                pairs.append(((x * SIDE + y) * CORES + core, (to_x * SIDE + to_y) * CORES + core))
    return pairs


def core_swap():
    return [(i, i ^ 1) for i in range(SIDE * SIDE * CORES)]


def shifted(value, stage):
    return [value] + [lax.ppermute(value, "row", chip_shifts(stage, step)) for step in STEP_ORDER]


def line_gathered(owned, after=(), specs=()):
    return joined(shifted(owned, 0), after, specs, (0, *STEP_ORDER))


def all_gathered(line, after=()):
    their_line = lax.ppermute(line, "row", core_swap())
    rest = joined(shifted(line, 1)[1:], (*after, their_line), (), [step - 1 for step in STEP_ORDER])
    their_rest = lax.ppermute(rest, "row", core_swap())
    return joined([line, rest, their_line, their_rest])


def padded_room(slots, span):
    step = GROUP * BATCH
    return (slots + span * (GROUP - 1) + step - 1) // step * step


def iota(shape, dim):
    return lax.broadcasted_iota(jnp.int32, shape, dim)


def plan_kernel(parts, owned, live_ref, rows_hbm, cols_hbm, center, half_width, _after, *refs):
    place_out, table_out, center_out, half_out, rows_ref, cols_ref, place_ref, table_ref, sems = refs
    pairs = ((rows_hbm, rows_ref), (cols_hbm, cols_ref))
    fetches = [pltpu.make_async_copy(source, target, sems.at[2 + k]) for k, (source, target) in enumerate(pairs)]
    for fetch in fetches:
        fetch.start()
    center_out[0] = center[...]
    half_out[0] = half_width[...]
    for fetch in fetches:
        fetch.wait()
    live = live_ref[0]
    me, here = lax.axis_index("row"), lax.axis_index("col")
    slots = rows_ref.shape[0]
    rows, cols = rows_ref[...].reshape(1, slots), cols_ref[...].reshape(1, slots)
    span = parts * owned
    lanes = LANES
    head = HEAD
    room = table_ref.shape[1] - head - SPARE

    turned = lax.rem(lax.div(rows, owned) + (parts - here), parts) * owned + lax.rem(rows, owned)
    ids = iota((1, slots), 1)
    alive = ids < live
    hot = jnp.where((turned == iota((span, slots), 0)) & alive, 1.0, 0.0)
    earlier = jnp.where(iota((slots, slots), 0) < iota((slots, slots), 1), 1.0, 0.0).astype(jnp.bfloat16)
    rank = jnp.dot(hot.astype(jnp.bfloat16), earlier, preferred_element_type=jnp.float32)
    counts = jnp.sum(hot, axis=1, keepdims=True).astype(jnp.int32)
    padded = lax.div(counts + (GROUP - 1), GROUP) * GROUP
    row_of, lane_of = iota((span, lanes), 0), iota((span, lanes), 1)
    across = jnp.sum(jnp.where(row_of == lane_of, padded, 0).astype(jnp.float32), axis=0, keepdims=True)
    starts = jnp.sum(jnp.where(lane_of < row_of, across, 0.0), axis=1, keepdims=True)
    ends = starts.astype(jnp.int32) + padded
    place = jnp.sum(hot * (rank + starts), axis=0, keepdims=True).astype(jnp.int32)
    place = jnp.where(alive, place, room + lax.rem(ids, CHUNK))
    place_ref[...] = place

    owner = lax.div(cols, owned)
    chip, my_chip = lax.div(owner, CORES), lax.div(me, CORES)
    dx = lax.rem(lax.div(my_chip, SIDE) + SIDE - lax.div(chip, SIDE), SIDE)
    dy = lax.rem(lax.rem(my_chip, SIDE) + SIDE - lax.rem(chip, SIDE), SIDE)
    dcore = lax.rem(me + owner, CORES)
    within = jnp.where(lax.rem(owner, CORES) == 0, dx * SIDE + dy, dy * SIDE + dx)
    source = (dcore * (SIDE * SIDE) + within) * owned + lax.rem(cols, owned)
    weights = jnp.broadcast_to(jnp.where(alive, source, 0).astype(jnp.float32), (8, slots)).astype(jnp.bfloat16)
    for block in range((room + SPARE) // SPARE):
        match = jnp.where(place == iota((SPARE, slots), 0) + block * SPARE, 1.0, 0.0).astype(jnp.bfloat16)
        found = lax.dot_general(weights, match, (((1,), (1,)), ((), ())), preferred_element_type=jnp.float32)
        table_ref[:, head + block * SPARE : head + (block + 1) * SPARE] = found[:1].astype(jnp.int32)

    ended = jnp.where(ends <= lane_of * GROUP, 1.0, 0.0)
    table_ref[:, lanes:head] = jnp.sum(ended, axis=0, keepdims=True).astype(jnp.int32)
    at_ends = jnp.sum(jnp.where(row_of == lane_of, ends, 0).astype(jnp.float32), axis=0, keepdims=True).astype(jnp.int32)
    lane = iota((1, lanes), 1)
    table_ref[:, :lanes] = jnp.where(lane == span, lax.div(live + (CHUNK - 1), CHUNK), at_ends)
    copies = [
        pltpu.make_async_copy(place_ref, place_out, sems.at[0]),
        pltpu.make_async_copy(table_ref, table_out, sems.at[1]),
    ]
    for copy in copies:
        copy.start()
    for copy in copies:
        copy.wait()


def sort_plan(rows, cols, live, scalars, after, parts, owned):
    slots = rows.shape[0]
    room = padded_room(slots, parts * owned)
    widths = (slots, HEAD + room + SPARE)
    anywhere = pl.BlockSpec(memory_space=pltpu.HBM)
    rows, cols = (pltpu.with_memory_space_constraint(a, pltpu.HBM) for a in (rows, cols))
    return pl.pallas_call(
        functools.partial(plan_kernel, parts, owned),
        out_shape=[pltpu.SMEM((1, width), jnp.int32) for width in widths] + [pltpu.SMEM((1,), jnp.float32)] * 2,
        in_specs=[SMEM, anywhere, anywhere, SMEM, SMEM, VMEM],
        out_specs=[SMEM] * 4,
        scratch_shapes=[pltpu.VMEM((slots,), jnp.int32)] * 2
        + [pltpu.VMEM((1, width), jnp.int32) for width in widths]
        + [pltpu.SemaphoreType.DMA((4,))],
        compiler_params=pltpu.CompilerParams(vmem_limit_bytes=8 * MIB),
        cost_estimate=pl.CostEstimate(flops=1000, bytes_accessed=1000, transcendentals=0),
    )(live, rows, cols, *scalars, after)


def prepare_kernel(span, place, sizes, _after, blocks_hbm, store, raw, sems):
    chunks = sizes[0, span]
    size = raw.shape[1]

    def copy_of(c):
        part = pl.ds(c * CHUNK, CHUNK)
        return pltpu.make_async_copy(blocks_hbm.at[part], raw.at[part], sems.at[c])

    @pl.loop(0, chunks)
    def _(c):
        copy_of(c).start()

    nothing = jnp.zeros((GROUP, size, size), store.dtype)

    @pl.loop(0, span)
    def _(row):
        store[pl.ds(jnp.maximum(sizes[0, row] - GROUP, 0), GROUP)] = nothing

    @pl.loop(0, chunks)
    def _(c):
        copy_of(c).wait()

        for u in range(CHUNK):
            slot = c * CHUNK + u
            store[place[0, slot]] = raw[slot].T


def prepared(place, sizes, blocks, after, span):
    slots, size, _ = blocks.shape
    return pl.pallas_call(
        functools.partial(prepare_kernel, span),
        out_shape=pltpu.VMEM((padded_room(slots, span) + SPARE, size, size), blocks.dtype),
        in_specs=[SMEM] * 2 + [VMEM, pl.BlockSpec(memory_space=pl.ANY)],
        out_specs=VMEM,
        scratch_shapes=[
            pltpu.VMEM((slots, size, size), blocks.dtype),
            pltpu.SemaphoreType.DMA((slots // CHUNK,)),
        ],
        compiler_params=pltpu.CompilerParams(vmem_limit_bytes=24 * MIB),
        cost_estimate=pl.CostEstimate(flops=1000, bytes_accessed=2 * slots * size * size, transcendentals=0),
    )(place, sizes, after, blocks)


def products_kernel(first_row, table, vec, store, *refs):
    out, sums = refs[-2:]
    owned = out.shape[0]
    size = store.shape[1]
    start = lax.div(table[0, first_row - 1], GROUP) if first_row else 0
    count = lax.div(table[0, first_row + owned - 1], GROUP) - start
    sums[...] = jnp.zeros_like(sums)

    @pl.loop(0, lax.div(count + (BATCH - 1), BATCH))
    def _(batch):
        for k in range(BATCH):
            group = start + batch * BATCH + k
            left = jnp.concatenate([vec[table[0, HEAD + group * GROUP + i]] for i in range(GROUP)], axis=1)
            right = store[pl.ds(group * GROUP, GROUP)].reshape(GROUP * size, size)
            sums[table[0, LANES + group]] += jnp.dot(left, right, preferred_element_type=jnp.float32)

    out[...] = sums[first_row : first_row + owned]


def local_products(part, vec, prep, after, owned, parts):
    table, store = prep
    _, vecs, size = vec.shape
    return pl.pallas_call(
        functools.partial(products_kernel, part * owned),
        out_shape=jax.ShapeDtypeStruct((owned, vecs, size), jnp.float32),
        in_specs=[SMEM] + [VMEM] * (2 + len(after)),
        out_specs=VMEM,
        scratch_shapes=[pltpu.VMEM((owned * parts + 1, vecs, size), jnp.float32)],
        compiler_params=pltpu.CompilerParams(vmem_limit_bytes=4 * MIB),
        cost_estimate=pl.CostEstimate(flops=640 // 2 * vecs * size * size, bytes_accessed=MIB, transcendentals=0),
    )(table, vec, kept(store), *after)


def kept(store):
    return pltpu.with_memory_space_constraint(store, pltpu.VMEM)


def first_kernel(center, half_width, current, *refs):
    pieces, (out, out_bf) = refs[:-2], refs[-2:]
    image = pieces[0][...]
    for piece in pieces[1:]:
        image += piece[...]
    value = (image - center[0] * current[...]) / half_width[0]
    out[...] = value
    out_bf[...] = value.astype(out_bf.dtype)


def next_kernel(count, center, half_width, current, previous, *refs):
    pieces, outs = refs[:count], refs[count:]
    image = pieces[0][...]
    for piece in pieces[1:]:
        image += piece[...]
    value = 2.0 * (image - center[0] * current[...]) / half_width[0] - previous[...]
    for out in outs:
        out[...] = value.astype(out.dtype)


def on_device(start_vectors, blocks, block_rows, block_cols, live_counts, center, half_width):
    parts = lax.axis_size("col")
    owned = start_vectors.shape[0]
    shape = start_vectors.shape
    scalars = (center, half_width)
    outs = (jax.ShapeDtypeStruct(shape, jnp.float32), jax.ShapeDtypeStruct(shape, jnp.bfloat16))

    def image_pieces(vec):
        pieces, last = [], ()
        for part in (*PART_ORDER, 0):
            piece = local_products(part, vec, prep, last, owned, parts)
            last = (piece,)
            if part:
                piece = lax.ppermute(piece, "col", [(i, (i + part) % parts) for i in range(parts)])
            pieces.append(piece)
        return pieces

    start_bf = rounded(start_vectors)
    place, table, *scalars = sort_plan(block_rows, block_cols, live_counts, scalars, start_bf, parts, owned)
    line = line_gathered(start_bf, (table,), (SMEM,))
    store = prepared(place, table, blocks, line, parts * owned)
    prep = (table, store)
    pieces = image_pieces(all_gathered(line, (kept(store),)))
    first = small_call(first_kernel, outs, [SMEM, SMEM] + [VMEM] * (1 + parts))
    current, current_bf = first(*scalars, start_vectors, *pieces)
    previous = start_vectors
    for turn in range(2):
        pieces = image_pieces(all_gathered(line_gathered(current_bf)))
        wanted = outs[:1] if turn else outs
        step = small_call(functools.partial(next_kernel, parts), wanted, [SMEM, SMEM] + [VMEM] * (2 + parts))
        following, *rest = step(*scalars, current, previous, *pieces)
        previous, current, current_bf = current, following, rest[0] if rest else None
    return current


def solution(mesh):
    return jax.shard_map(
        on_device,
        mesh=mesh,
        in_specs=(
            P(("row", "col"), None, None),
            P(("row", "col"), None, None),
            P(("row", "col")),
            P(("row", "col")),
            P(("row", "col")),
            P(),
            P(),
        ),
        out_specs=P(("row", "col"), None, None),
        check_vma=False,
    )
```

```python
import functools

import jax
import jax.numpy as jnp
from jax import lax
from jax.experimental import pallas as pl
from jax.experimental.pallas import tpu as pltpu
from jax.sharding import PartitionSpec as P


SIDE = 4
CORES = 2
CHUNK = 32
SPARE = 64
GROUP = 4
BATCH = 24
LANES = 256
HEAD = 2 * LANES
PART_ORDER = (2, 1, 3)
STEP_ORDER = (1, 3, 2)
MIB = 1 << 20


VMEM = pl.BlockSpec(memory_space=pltpu.VMEM)
SMEM = pl.BlockSpec(memory_space=pltpu.SMEM)


def small_call(kernel, outs, in_specs, flops=1000):
    cost = pl.CostEstimate(flops=flops, bytes_accessed=1000, transcendentals=0)
    return pl.pallas_call(
        kernel,
        out_shape=outs,
        in_specs=in_specs,
        out_specs=jax.tree.map(lambda _: VMEM, outs),
        compiler_params=pltpu.CompilerParams(vmem_limit_bytes=4 * MIB),
        cost_estimate=cost,
    )


def join_kernel(places, *refs):
    parts, out = refs[: len(places)], refs[-1]
    size = parts[0].shape[0]
    for place, part in zip(places, parts):
        out[place * size : (place + 1) * size] = part[...]


def joined(parts, after=(), after_specs=(), places=(0, 1)):
    shape = (len(parts) * parts[0].shape[0], *parts[0].shape[1:])
    kernel = functools.partial(join_kernel, places)
    specs = [VMEM] * len(parts) + list(after_specs or [VMEM] * len(after))
    return small_call(kernel, jax.ShapeDtypeStruct(shape, parts[0].dtype), specs)(*parts, *after)


def round_kernel(value, out):
    out[...] = value[...].astype(out.dtype)


def rounded(value):
    return small_call(round_kernel, jax.ShapeDtypeStruct(value.shape, jnp.bfloat16), [VMEM])(value)


def chip_shifts(stage, step):
    pairs = []
    for x in range(SIDE):
        for y in range(SIDE):
            for core in range(CORES):
                along_y = stage == core
                to_x = x if along_y else (x + step) % SIDE
                to_y = (y + step) % SIDE if along_y else y
                pairs.append(((x * SIDE + y) * CORES + core, (to_x * SIDE + to_y) * CORES + core))
    return pairs


def core_swap():
    return [(i, i ^ 1) for i in range(SIDE * SIDE * CORES)]


def shifted(value, stage):
    return [value] + [lax.ppermute(value, "row", chip_shifts(stage, step)) for step in STEP_ORDER]


def line_gathered(owned, after=(), specs=()):
    return joined(shifted(owned, 0), after, specs, (0, *STEP_ORDER))


def all_gathered(line, after=()):
    mine = joined(shifted(line, 1), after, (), (0, *STEP_ORDER))
    return joined([mine, lax.ppermute(mine, "row", core_swap())])


def padded_room(slots, span):
    step = GROUP * BATCH
    return (slots + span * (GROUP - 1) + step - 1) // step * step


def iota(shape, dim):
    return lax.broadcasted_iota(jnp.int32, shape, dim)


def plan_kernel(parts, owned, live_ref, rows_hbm, cols_hbm, center, half_width, _after, *refs):
    place_out, table_out, center_out, half_out, rows_ref, cols_ref, place_ref, table_ref, sems = refs
    pairs = ((rows_hbm, rows_ref), (cols_hbm, cols_ref))
    fetches = [pltpu.make_async_copy(source, target, sems.at[2 + k]) for k, (source, target) in enumerate(pairs)]
    for fetch in fetches:
        fetch.start()
    center_out[0] = center[...]
    half_out[0] = half_width[...]
    for fetch in fetches:
        fetch.wait()
    live = live_ref[0]
    me, here = lax.axis_index("row"), lax.axis_index("col")
    slots = rows_ref.shape[0]
    rows, cols = rows_ref[...].reshape(1, slots), cols_ref[...].reshape(1, slots)
    span = parts * owned
    lanes = LANES
    head = HEAD
    room = table_ref.shape[1] - head - SPARE

    away = lax.rem(lax.div(rows, owned) + (parts - here), parts)
    spot = sum(jnp.where(away == part, k, 0) for k, part in enumerate((*PART_ORDER, 0)))
    turned = spot * owned + lax.rem(rows, owned)
    ids = iota((1, slots), 1)
    alive = ids < live
    hot = jnp.where((turned == iota((span, slots), 0)) & alive, 1.0, 0.0)
    earlier = jnp.where(iota((slots, slots), 0) < iota((slots, slots), 1), 1.0, 0.0).astype(jnp.bfloat16)
    rank = jnp.dot(hot.astype(jnp.bfloat16), earlier, preferred_element_type=jnp.float32)
    counts = jnp.sum(hot, axis=1, keepdims=True).astype(jnp.int32)
    padded = lax.div(counts + (GROUP - 1), GROUP) * GROUP
    row_of, lane_of = iota((span, lanes), 0), iota((span, lanes), 1)
    across = jnp.sum(jnp.where(row_of == lane_of, padded, 0).astype(jnp.float32), axis=0, keepdims=True)
    starts = jnp.sum(jnp.where(lane_of < row_of, across, 0.0), axis=1, keepdims=True)
    ends = starts.astype(jnp.int32) + padded
    place = jnp.sum(hot * (rank + starts), axis=0, keepdims=True).astype(jnp.int32)
    place = jnp.where(alive, place, room + lax.rem(ids, CHUNK))
    place_ref[...] = place

    owner = lax.div(cols, owned)
    chip, my_chip = lax.div(owner, CORES), lax.div(me, CORES)
    dx = lax.rem(lax.div(my_chip, SIDE) + SIDE - lax.div(chip, SIDE), SIDE)
    dy = lax.rem(lax.rem(my_chip, SIDE) + SIDE - lax.rem(chip, SIDE), SIDE)
    dcore = lax.rem(me + owner, CORES)
    within = jnp.where(lax.rem(owner, CORES) == 0, dx * SIDE + dy, dy * SIDE + dx)
    source = (dcore * (SIDE * SIDE) + within) * owned + lax.rem(cols, owned)
    weights = jnp.broadcast_to(jnp.where(alive, source, 0).astype(jnp.float32), (8, slots)).astype(jnp.bfloat16)
    for block in range((room + SPARE) // SPARE):
        match = jnp.where(place == iota((SPARE, slots), 0) + block * SPARE, 1.0, 0.0).astype(jnp.bfloat16)
        found = lax.dot_general(weights, match, (((1,), (1,)), ((), ())), preferred_element_type=jnp.float32)
        table_ref[:, head + block * SPARE : head + (block + 1) * SPARE] = found[:1].astype(jnp.int32)

    ended = jnp.where(ends <= lane_of * GROUP, 1.0, 0.0)
    table_ref[:, lanes:head] = jnp.sum(ended, axis=0, keepdims=True).astype(jnp.int32)
    at_ends = jnp.sum(jnp.where(row_of == lane_of, ends, 0).astype(jnp.float32), axis=0, keepdims=True).astype(jnp.int32)
    lane = iota((1, lanes), 1)
    table_ref[:, :lanes] = jnp.where(lane == span, lax.div(live + (CHUNK - 1), CHUNK), at_ends)
    copies = [
        pltpu.make_async_copy(place_ref, place_out, sems.at[0]),
        pltpu.make_async_copy(table_ref, table_out, sems.at[1]),
    ]
    for copy in copies:
        copy.start()
    for copy in copies:
        copy.wait()


def sort_plan(rows, cols, live, scalars, after, parts, owned):
    slots = rows.shape[0]
    room = padded_room(slots, parts * owned)
    widths = (slots, HEAD + room + SPARE)
    anywhere = pl.BlockSpec(memory_space=pltpu.HBM)
    rows, cols = (pltpu.with_memory_space_constraint(a, pltpu.HBM) for a in (rows, cols))
    return pl.pallas_call(
        functools.partial(plan_kernel, parts, owned),
        out_shape=[pltpu.SMEM((1, width), jnp.int32) for width in widths] + [pltpu.SMEM((1,), jnp.float32)] * 2,
        in_specs=[SMEM, anywhere, anywhere, SMEM, SMEM, VMEM],
        out_specs=[SMEM] * 4,
        scratch_shapes=[pltpu.VMEM((slots,), jnp.int32)] * 2
        + [pltpu.VMEM((1, width), jnp.int32) for width in widths]
        + [pltpu.SemaphoreType.DMA((4,))],
        compiler_params=pltpu.CompilerParams(vmem_limit_bytes=8 * MIB),
        cost_estimate=pl.CostEstimate(flops=1000, bytes_accessed=1000, transcendentals=0),
    )(live, rows, cols, *scalars, after)


def prepare_kernel(span, place, sizes, _after, blocks_hbm, store, raw, sems):
    chunks = sizes[0, span]
    size = raw.shape[1]

    def copy_of(c):
        part = pl.ds(c * CHUNK, CHUNK)
        return pltpu.make_async_copy(blocks_hbm.at[part], raw.at[part], sems.at[c])

    @pl.loop(0, chunks)
    def _(c):
        copy_of(c).start()

    nothing = jnp.zeros((GROUP, size, size), store.dtype)

    @pl.loop(0, span)
    def _(row):
        store[pl.ds(jnp.maximum(sizes[0, row] - GROUP, 0), GROUP)] = nothing

    @pl.loop(0, chunks)
    def _(c):
        copy_of(c).wait()

        for u in range(CHUNK):
            slot = c * CHUNK + u
            store[place[0, slot]] = raw[slot].T


def prepared(place, sizes, blocks, after, span):
    slots, size, _ = blocks.shape
    return pl.pallas_call(
        functools.partial(prepare_kernel, span),
        out_shape=pltpu.VMEM((padded_room(slots, span) + SPARE, size, size), blocks.dtype),
        in_specs=[SMEM] * 2 + [VMEM, pl.BlockSpec(memory_space=pl.ANY)],
        out_specs=VMEM,
        scratch_shapes=[
            pltpu.VMEM((slots, size, size), blocks.dtype),
            pltpu.SemaphoreType.DMA((slots // CHUNK,)),
        ],
        compiler_params=pltpu.CompilerParams(vmem_limit_bytes=24 * MIB),
        cost_estimate=pl.CostEstimate(flops=1000, bytes_accessed=2 * slots * size * size, transcendentals=0),
    )(place, sizes, after, blocks)


def products_kernel(first_row, count_out, table, vec, store, *refs):
    outs, sums = refs[-1 - count_out : -1], refs[-1]
    owned = outs[0].shape[0]
    size = store.shape[1]
    start = lax.div(table[0, first_row - 1], GROUP) if first_row else 0
    count = lax.div(table[0, first_row + count_out * owned - 1], GROUP) - start
    sums[...] = jnp.zeros_like(sums)

    @pl.loop(0, lax.div(count + (BATCH - 1), BATCH))
    def _(batch):
        for k in range(BATCH):
            group = start + batch * BATCH + k
            left = jnp.concatenate([vec[table[0, HEAD + group * GROUP + i]] for i in range(GROUP)], axis=1)
            right = store[pl.ds(group * GROUP, GROUP)].reshape(GROUP * size, size)
            sums[table[0, LANES + group]] += jnp.dot(left, right, preferred_element_type=jnp.float32)

    for k, out in enumerate(outs):
        out[...] = sums[first_row + k * owned : first_row + (k + 1) * owned]


def local_products(spot, count, vec, prep, after, owned, parts):
    table, store = prep
    _, vecs, size = vec.shape
    return pl.pallas_call(
        functools.partial(products_kernel, spot * owned, count),
        out_shape=[jax.ShapeDtypeStruct((owned, vecs, size), jnp.float32)] * count,
        in_specs=[SMEM] + [VMEM] * (2 + len(after)),
        out_specs=[VMEM] * count,
        scratch_shapes=[pltpu.VMEM((owned * parts + 1, vecs, size), jnp.float32)],
        compiler_params=pltpu.CompilerParams(vmem_limit_bytes=4 * MIB),
        cost_estimate=pl.CostEstimate(flops=640 // 2 * vecs * size * size, bytes_accessed=MIB, transcendentals=0),
    )(table, vec, kept(store), *after)


def kept(store):
    return pltpu.with_memory_space_constraint(store, pltpu.VMEM)


def first_kernel(center, half_width, current, *refs):
    pieces, (out, out_bf) = refs[:-2], refs[-2:]
    image = pieces[0][...]
    for piece in pieces[1:]:
        image += piece[...]
    value = (image - center[0] * current[...]) / half_width[0]
    out[...] = value
    out_bf[...] = value.astype(out_bf.dtype)


def next_kernel(count, center, half_width, current, previous, *refs):
    pieces, outs = refs[:count], refs[count:]
    image = pieces[0][...]
    for piece in pieces[1:]:
        image += piece[...]
    value = 2.0 * (image - center[0] * current[...]) / half_width[0] - previous[...]
    for out in outs:
        out[...] = value.astype(out.dtype)


def on_device(start_vectors, blocks, block_rows, block_cols, live_counts, center, half_width):
    parts = lax.axis_size("col")
    owned = start_vectors.shape[0]
    shape = start_vectors.shape
    scalars = (center, half_width)
    outs = (jax.ShapeDtypeStruct(shape, jnp.float32), jax.ShapeDtypeStruct(shape, jnp.bfloat16))

    def image_pieces(vec):
        pieces, last = [], ()
        for spot, aways in ((0, PART_ORDER[:1]), (1, PART_ORDER[1:]), (parts - 1, ())):
            last = local_products(spot, max(1, len(aways)), vec, prep, last[:1], owned, parts)
            if not aways:
                pieces.append(last[0])
            for away, piece in zip(aways, last):
                pieces.append(lax.ppermute(piece, "col", [(i, (i + away) % parts) for i in range(parts)]))
        return pieces[::-1]

    start_bf = rounded(start_vectors)
    place, table, *scalars = sort_plan(block_rows, block_cols, live_counts, scalars, start_bf, parts, owned)
    line = line_gathered(start_bf, (table,), (SMEM,))
    store = prepared(place, table, blocks, line, parts * owned)
    prep = (table, store)
    pieces = image_pieces(all_gathered(line, (kept(store),)))
    first = small_call(first_kernel, outs, [SMEM, SMEM] + [VMEM] * (1 + parts))
    current, current_bf = first(*scalars, start_vectors, *pieces)
    previous = start_vectors
    for turn in range(2):
        pieces = image_pieces(all_gathered(line_gathered(current_bf)))
        wanted = outs[:1] if turn else outs
        step = small_call(functools.partial(next_kernel, parts), wanted, [SMEM, SMEM] + [VMEM] * (2 + parts))
        following, *rest = step(*scalars, current, previous, *pieces)
        previous, current, current_bf = current, following, rest[0] if rest else None
    return current


def solution(mesh):
    return jax.shard_map(
        on_device,
        mesh=mesh,
        in_specs=(
            P(("row", "col"), None, None),
            P(("row", "col"), None, None),
            P(("row", "col")),
            P(("row", "col")),
            P(("row", "col")),
            P(),
            P(),
        ),
        out_specs=P(("row", "col"), None, None),
        check_vma=False,
    )
```
